256 devices in a mesh: ep: 128 (over y, x, z), rep: 2 (over core).
Axes of the slice: x: 4, y: 4, z: 8, core: 2. Of those that a mesh axis runs over, the one named last changes fastest.
Arguments:
- dy: bfloat16 [4096, 2048], P('ep'), may hold values from -6 to 6
- probs: float32 [4096, 8], P('ep'), may hold values from 0.02 to 0.5
- expert_ids: int32 [4096, 8], P('ep'), may hold values from 0 to 127, as said below
- copy_choice: int32 [4096, 8], P('ep'), may hold values from 0 to 1, as said below
- saved_inputs: bfloat16 [128, 2, 128, 2, 2048], P('ep', 'rep'), may hold values from -24 to 24
- saved_gate: bfloat16 [128, 2, 128, 2, 768], P('ep', 'rep'), may hold values from -4 to 4
- saved_up: bfloat16 [128, 2, 128, 2, 768], P('ep', 'rep'), may hold values from -12 to 12
- down_weight: bfloat16 [128, 768, 2048], P('ep', None, 'rep'), may hold values from -4 to 4
- gate_weight: bfloat16 [128, 2048, 768], P('ep', 'rep'), may hold values from -4 to 4
- up_weight: bfloat16 [128, 2048, 768], P('ep', 'rep'), may hold values from -4 to 4
- new_owner: int32 [128], replicated, may hold values from 0 to 127, each once
Outputs:
- new_gate: bfloat16 [128, 2048, 768], P('ep', 'rep')
- new_up: bfloat16 [128, 2048, 768], P('ep', 'rep')
The draws below stay inside these ranges and needn't reach their ends.
Inputs may be any that keep to these rules, and one draw needn't show every extreme that they name: `expert_ids`: each row names 8 different experts; the rows of one index of ep name each expert at most 2 * 2 times. `copy_choice`: of the pairs of the rows of one index of ep that name one expert, at most 2 take each copy; some take exactly 2 in every draw. `new_owner`: each expert has exactly one owner.
All inputs are finite; a program needn't handle non-finite values.
Results may differ from the reference program's by a relative error of at most 0.0056.
Values may be sent and summed in bfloat16 or wider, within the bound.
A program may use at most 64 MiB of HBM per device.

```python
import math
import jax
import jax.numpy as jnp
from jax import lax

D = 2048
F = 768
TOP = 8
EXPERTS = 128
COPIES = 2
TOK_EP = 32
TOKENS = 4096
MC = 2
ITERS = 2
N_EP = 128


def make_routing(key):
    base_key = jax.random.fold_in(key, 5)
    pair_key, shift_key, parity_key, token_key = jax.random.split(base_key, 4)
    block_count = TOKENS // TOK_EP
    halfway = EXPERTS // 2
    pair_block = TOK_EP * TOP
    order = jax.random.permutation(pair_key, EXPERTS)
    shifts = jax.random.randint(shift_key, (block_count, halfway), 0, MC + 1)
    forced = jnp.arange(halfway)[None, :] == (jnp.arange(block_count) % halfway)[:, None]
    shifts = jnp.where(forced, MC, shifts)
    delta = jnp.zeros((block_count, EXPERTS), jnp.int32)
    delta = delta.at[:, order[:halfway]].set(shifts).at[:, order[halfway:]].set(-shifts)
    counts = MC + delta
    ends = jnp.cumsum(counts, axis=1)
    starts = ends - counts
    position = jnp.arange(pair_block, dtype=jnp.int32)
    expert_at = jnp.sum((ends[:, None, :] <= position[None, :, None]).astype(jnp.int32), axis=2)
    start_at = jnp.take_along_axis(starts, expert_at, axis=1)
    parity = jax.random.randint(parity_key, (block_count, EXPERTS), 0, 2)
    copy_at = (position[None, :] - start_at + jnp.take_along_axis(parity, expert_at, axis=1)) % 2
    ids_grid = expert_at.reshape(block_count, TOP, TOK_EP).transpose(0, 2, 1)
    copy_grid = copy_at.reshape(block_count, TOP, TOK_EP).transpose(0, 2, 1)
    shuffles = jax.vmap(lambda block_key: jax.random.permutation(block_key, TOK_EP))(jax.random.split(token_key, block_count))
    index = jnp.broadcast_to(shuffles[:, :, None], ids_grid.shape)
    ids_grid = jnp.take_along_axis(ids_grid, index, axis=1)
    copy_grid = jnp.take_along_axis(copy_grid, index, axis=1)
    return (ids_grid.reshape(TOKENS, TOP).astype(jnp.int32), copy_grid.reshape(TOKENS, TOP).astype(jnp.int32))


def draw_expert_ids(key, part):
    return make_routing(key)[0]


def draw_copy_choice(key, part):
    return make_routing(key)[1]


def draw_saved_inputs(key, part):
    first_key, column_key, row_key = jax.random.split(jax.random.fold_in(key, 11), 3)
    shape = (EXPERTS, COPIES, EXPERTS, MC, D)
    column_scale = jnp.exp(jax.random.uniform(column_key, (D,), minval=math.log(0.3), maxval=math.log(3.0)))
    row_scale = jnp.exp(jax.random.uniform(row_key, (EXPERTS, COPIES, EXPERTS, MC, 1), minval=math.log(0.5), maxval=math.log(2.0)))
    values = jax.random.truncated_normal(first_key, -4.0, 4.0, shape)
    return (values * column_scale * row_scale).astype(jnp.bfloat16)


def draw_saved_up(key, part):
    first_key, column_key = jax.random.split(jax.random.fold_in(key, 13), 2)
    shape = (EXPERTS, COPIES, EXPERTS, MC, F)
    column_scale = jnp.exp(jax.random.uniform(column_key, (F,), minval=math.log(0.3), maxval=math.log(3.0)))
    values = jax.random.truncated_normal(first_key, -4.0, 4.0, shape)
    return (values * column_scale).astype(jnp.bfloat16)


def steps_of(rng, extent, pieces, least, high):
    level = 1.0
    for dim, blocks in pieces:
        heights = jax.random.uniform(jax.random.fold_in(jax.random.fold_in(rng, 6), dim), (blocks,), jnp.float32, least / len(pieces), high / len(pieces))
        level = level * jnp.repeat(jnp.exp(heights), extent[dim] // blocks).reshape((-1,) + (1,) * (len(extent) - 1 - dim))
    return level


def bell_draw(stream_key, extent, deviation, reach, pieces=(), kind=jnp.bfloat16):
    array = deviation * jax.random.normal(stream_key, extent, jnp.float32)
    if pieces:
        array = array * steps_of(stream_key, extent, pieces, -0.22, 0.18)
    return jnp.clip(array, -reach, reach).astype(kind)


def setup_inputs(seed: int = 0) -> dict:
    key_of = jax.random.split(jax.random.key(seed), 12)
    dy = bell_draw(key_of[0], (TOKENS, D), 1.0, 6.0, ((0, 128),))
    probs = jnp.clip(jnp.exp(math.log(0.5) - 3.218876 * jax.random.uniform(key_of[1], (TOKENS, TOP), jnp.float32) ** steps_of(key_of[1], (TOKENS, TOP), ((0, 128),), -0.2, 0.2)), 0.02, 0.5)
    expert_ids = draw_expert_ids(jax.random.fold_in(key_of[11], 71), 0)
    copy_choice = draw_copy_choice(jax.random.fold_in(key_of[11], 71), 0)
    saved_inputs = draw_saved_inputs(jax.random.fold_in(key_of[11], 71), 0)
    saved_gate = bell_draw(key_of[5], (EXPERTS, COPIES, N_EP, MC, F), 1.0, 4.0, ((0, 128), (1, 2)))
    saved_up = draw_saved_up(jax.random.fold_in(key_of[11], 71), 0)
    down_weight = bell_draw(key_of[7], (EXPERTS, F, D), 1.0, 4.0, ((0, 128), (2, 2)))
    gate_weight = bell_draw(key_of[8], (EXPERTS, D, F), 1.0, 4.0, ((0, 128), (1, 2)))
    up_weight = bell_draw(key_of[9], (EXPERTS, D, F), 1.0, 4.0, ((0, 128), (1, 2)))
    new_owner = jax.random.permutation(key_of[10], EXPERTS).astype(jnp.int32)
    return dict(dy=dy, probs=probs, expert_ids=expert_ids, copy_choice=copy_choice, saved_inputs=saved_inputs, saved_gate=saved_gate, saved_up=saved_up, down_weight=down_weight, gate_weight=gate_weight, up_weight=up_weight, new_owner=new_owner)


quintic_first = 3.4445
quintic_second = -4.775
quintic_third = 2.0315
step_scale = 2.0
epsilon = 1e-07

def contract_rows(left, right):
    return lax.dot_general(left, right, (((0,), (0,)), ((), ())), preferred_element_type=jnp.float32)

def orthogonalize(gradient):
    total = jnp.sqrt(jnp.sum(gradient * gradient))
    iterate = lax.optimization_barrier((gradient / (total + epsilon)).astype(jnp.bfloat16))
    for repeat in range(ITERS):
        gram = lax.optimization_barrier(contract_rows(iterate, iterate).astype(jnp.bfloat16))
        square = jnp.dot(gram, gram, preferred_element_type=jnp.float32)
        poly = (quintic_second * gram.astype(jnp.float32) + quintic_third * square).astype(jnp.bfloat16)
        mixed = quintic_first * iterate.astype(jnp.float32) + jnp.dot(iterate, poly, preferred_element_type=jnp.float32)
        iterate = lax.optimization_barrier(mixed.astype(jnp.bfloat16))
    return iterate

def slot_numbers(expert_ids, copy_choice):
    pair_block = TOK_EP * TOP
    block_count = expert_ids.shape[0] // TOK_EP
    keyed = (expert_ids * COPIES + copy_choice).reshape(block_count, pair_block)
    matches = (keyed[:, :, None] == jnp.arange(EXPERTS * COPIES, dtype=jnp.int32)[None, None, :]).astype(jnp.int32)
    return (lax.optimization_barrier(jnp.sum(jnp.cumsum(matches, axis=1) * matches, axis=2)) - 1).reshape(-1).astype(jnp.int32)

def expert_update(operands):
    routed_rows, inputs, pre_gate, pre_up, down_matrix, gate_matrix, up_matrix = operands
    hidden_grad = lax.dot_general(routed_rows, down_matrix, (((1,), (1,)), ((), ())), preferred_element_type=jnp.float32) / math.sqrt(F)
    gate_value = pre_gate.astype(jnp.float32)
    up_value = pre_up.astype(jnp.float32)
    sigmoid = jax.nn.sigmoid(gate_value)
    gate_rows = (hidden_grad * up_value * sigmoid * (1.0 + gate_value * (1.0 - sigmoid))).astype(jnp.bfloat16)
    up_rows = (hidden_grad * gate_value * sigmoid).astype(jnp.bfloat16)
    grad_gate = contract_rows(inputs, gate_rows)
    grad_up = contract_rows(inputs, up_rows)
    factor = step_scale * math.sqrt(D)
    new_gate = (gate_matrix.astype(jnp.float32) - factor * orthogonalize(grad_gate).astype(jnp.float32)).astype(jnp.bfloat16)
    new_up = (up_matrix.astype(jnp.float32) - factor * orthogonalize(grad_up).astype(jnp.float32)).astype(jnp.bfloat16)
    return (new_gate, new_up)

def reference(dy, probs, expert_ids, copy_choice, saved_inputs, saved_gate, saved_up, down_weight, gate_weight, up_weight, new_owner):
    pair_total = TOKENS * TOP
    slots = slot_numbers(expert_ids, copy_choice)
    flat_ids = expert_ids.reshape(-1).astype(jnp.int32)
    flat_copy = copy_choice.reshape(-1).astype(jnp.int32)
    source = jnp.arange(pair_total, dtype=jnp.int32) // (TOK_EP * TOP)
    target = ((flat_ids * COPIES + flat_copy) * N_EP + source) * MC + slots
    scaled = (probs[:, :, None] * dy.astype(jnp.float32)[:, None, :]).astype(jnp.bfloat16).reshape(pair_total, D)
    routed = jnp.zeros((EXPERTS * COPIES * N_EP * MC, D), jnp.bfloat16).at[target].set(scaled)
    routed = routed.reshape(EXPERTS, COPIES * N_EP * MC, D)
    gate_moved, up_moved = lax.map(expert_update, (routed, saved_inputs.reshape(EXPERTS, -1, D), saved_gate.reshape(EXPERTS, -1, F), saved_up.reshape(EXPERTS, -1, F), down_weight, gate_weight, up_weight))
    new_gate = jnp.zeros_like(gate_weight).at[new_owner].set(gate_moved)
    new_up = jnp.zeros_like(up_weight).at[new_owner].set(up_moved)
    return (new_gate, new_up)
```

```python
import functools
import math

import jax
import jax.numpy as jnp
from jax import lax
from jax.experimental import pallas as pl
from jax.experimental.pallas import tpu as pltpu
from jax.sharding import PartitionSpec as P

MESH = pl.DeviceIdType.MESH
ITERS = 2

quintic_first = 3.4445
quintic_second = -4.775
quintic_third = 2.0315
step_scale = 2.0
epsilon = 1e-07

GRID = (4, 4, 8)


def shifted(me, k):
    ny, nx, nz = GRID
    y, x, z = me // (nx * nz), (me // nz) % nx, me % nz
    dy, dx, dz = k // (nx * nz), (k // nz) % nx, k % nz
    return (lax.rem(y + dy, ny) * nx + lax.rem(x + dx, nx)) * nz + lax.rem(z + dz, nz)


def greet(n, me):
    barrier = pltpu.get_barrier_semaphore()

    def say(k, carry):
        pl.semaphore_signal(barrier, inc=1, device_id={"ep": shifted(me, k)}, device_id_type=MESH)
        return carry

    lax.fori_loop(1, n, say, 0)
    pl.semaphore_wait(barrier, n - 1)


def from_partner(block):
    return lax.ppermute(block, "rep", [(0, 1), (1, 0)])


def dot(a, b, dims):
    return lax.dot_general(a, b, (dims, ((), ())), preferred_element_type=jnp.float32)


def exchange_kernel(n, x_ref, o_ref, send, recv, local):
    me = lax.axis_index("ep")
    greet(n, me)
    own = pltpu.make_async_copy(x_ref.at[me], o_ref.at[me], local)
    own.start()

    def go(k, carry):
        to = shifted(me, k)
        pltpu.make_async_remote_copy(
            src_ref=x_ref.at[to], dst_ref=o_ref.at[me], send_sem=send, recv_sem=recv,
            device_id={"ep": to}, device_id_type=MESH,
        ).start()
        return carry

    lax.fori_loop(1, n, go, 0)
    own.wait()
    rest = pl.ds(0, n - 1)
    everything = pltpu.make_async_remote_copy(
        src_ref=x_ref.at[rest], dst_ref=o_ref.at[rest], send_sem=send, recv_sem=recv,
        device_id={"ep": shifted(me, 1)}, device_id_type=MESH,
    )
    everything.wait_send()
    everything.wait_recv()


def exchange(x):
    n = x.shape[0]
    return pl.pallas_call(
        functools.partial(exchange_kernel, n),
        out_shape=jax.ShapeDtypeStruct(x.shape, x.dtype),
        in_specs=[pl.BlockSpec(memory_space=pl.ANY)],
        out_specs=pl.BlockSpec(memory_space=pl.ANY),
        scratch_shapes=[pltpu.SemaphoreType.DMA] * 3,
        compiler_params=pltpu.CompilerParams(collective_id=1, has_side_effects=True),
        name="exchange",
    )(x)


def orthogonal_factor(kernel_matrix, rows):
    high = kernel_matrix.astype(jnp.bfloat16)
    low = (kernel_matrix - high.astype(jnp.float32)).astype(jnp.bfloat16)
    product = dot(high, rows, ((1,), (0,))) + dot(low, rows, ((1,), (0,)))
    total = jnp.sqrt(jnp.maximum(jnp.sum(rows.astype(jnp.float32) * product), 0.0))
    scale = 1.0 / (total + epsilon)
    product = product * (scale * scale)
    for repeat in range(ITERS):
        if repeat:
            product = dot(high, rows, ((1,), (0,))) + dot(low, rows, ((1,), (0,)))
        gram = dot(rows, product.astype(jnp.bfloat16), ((0,), (0,)))
        half = gram.astype(jnp.bfloat16)
        square = dot(half, half, ((1,), (0,)))
        poly = (quintic_second * gram + quintic_third * square).astype(jnp.bfloat16)
        mixed = quintic_first * rows.astype(jnp.float32) + dot(rows, poly, ((1,), (0,)))
        if not repeat:
            mixed = mixed * scale
        rows = mixed.astype(jnp.bfloat16)
    return rows


def move_kernel(
    n, factor, inverse, k_ref, r_ref, x_ref, gate_ref, up_ref, own_out, other_out,
    weights, factors, made0, made1, held0, held1, ready0, ready1, load, send, recv, local, swap,
):
    me = lax.axis_index("ep")
    core = lax.axis_index("rep")
    outs, made, held, ready = (own_out, other_out), (made0, made1), (held0, held1), (ready0, ready1)
    ny = GRID[0]
    group = n // ny
    piece = weights.shape[1] // n
    block = group * piece
    rest = pl.ds(0, n - 1)
    partner = {"rep": 1 - core}

    barrier = pltpu.get_barrier_semaphore()

    def say(k, carry):
        pl.semaphore_signal(barrier, inc=1, device_id={"ep": shifted(me, k)}, device_id_type=MESH)
        return carry

    lax.fori_loop(1, n, say, 0)
    pl.semaphore_signal(barrier, inc=1, device_id=partner, device_id_type=MESH)

    for c, refs in enumerate(((gate_ref, up_ref), (up_ref, gate_ref))):
        @pl.when(core == c)
        def _(refs=refs):
            for q in range(2):
                pltpu.make_async_copy(refs[q], weights.at[q], load.at[q]).start()

    factors[0] = orthogonal_factor(k_ref[...], r_ref[...])
    pl.semaphore_wait(barrier, n)
    trade = pltpu.make_async_remote_copy(
        src_ref=factors.at[0], dst_ref=factors.at[1], send_sem=swap.at[0], recv_sem=swap.at[1],
        device_id=partner, device_id_type=MESH,
    )
    trade.start()

    for q in range(2):
        pltpu.make_async_copy(gate_ref, weights.at[q], load.at[q]).wait()
        if q:
            trade.wait_recv()

        def spread(k, carry, q=q):
            to = shifted(me, k)
            pltpu.make_async_remote_copy(
                src_ref=made[q].at[to], dst_ref=held[q].at[me], send_sem=send.at[q], recv_sem=recv.at[q],
                device_id={"ep": to}, device_id_type=MESH,
            ).start()
            return carry

        def produce(dy, carry, q=q):
            y = lax.rem(me // group + dy, ny)
            rows = pl.ds(pl.multiple_of(y * block, block), block)
            ortho = dot(x_ref[:, rows], factors[q], ((0,), (0,)))
            fresh = (weights[q, rows, :].astype(jnp.float32) - factor * ortho).astype(jnp.bfloat16)
            made[q][pl.ds(y * group, group)] = fresh.reshape(group, piece, fresh.shape[1])
            lax.fori_loop(jnp.where(dy == 0, 1, dy * group), (dy + 1) * group, spread, 0)
            return carry

        lax.fori_loop(0, ny, produce, 0)
        pltpu.make_async_copy(made[q].at[me], held[q].at[me], local.at[q]).start()

    for q in range(2):
        pltpu.make_async_copy(made[q].at[me], held[q].at[me], local.at[q]).wait()
        pltpu.make_async_remote_copy(
            src_ref=made[q].at[rest], dst_ref=held[q].at[rest], send_sem=send.at[q], recv_sem=recv.at[q],
            device_id={"ep": shifted(me, 1)}, device_id_type=MESH,
        ).wait_recv()

        def collect(k, carry, q=q):
            to = shifted(me, k)
            ready[q][k] = held[q][inverse[to]]
            pltpu.make_async_remote_copy(
                src_ref=ready[q].at[k], dst_ref=outs[q].at[me], send_sem=send.at[2 + q], recv_sem=recv.at[2 + q],
                device_id={"ep": to}, device_id_type=MESH,
            ).start()
            return carry

        lax.fori_loop(1, n, collect, 0)
        ready[q][0] = held[q][inverse[me]]
        pltpu.make_async_copy(ready[q].at[0], outs[q].at[me], local.at[2 + q]).start()

    trade.wait_send()
    for q in range(2):
        pltpu.make_async_copy(ready[q].at[0], outs[q].at[me], local.at[2 + q]).wait()
        pltpu.make_async_remote_copy(
            src_ref=made[q].at[rest], dst_ref=held[q].at[rest], send_sem=send.at[q], recv_sem=recv.at[q],
            device_id={"ep": shifted(me, 1)}, device_id_type=MESH,
        ).wait_send()
        last = pltpu.make_async_remote_copy(
            src_ref=ready[q].at[rest], dst_ref=outs[q].at[rest], send_sem=send.at[2 + q], recv_sem=recv.at[2 + q],
            device_id={"ep": shifted(me, 1)}, device_id_type=MESH,
        )
        last.wait_send()
        last.wait_recv()


def move(n, factor, inverse, kernel_matrix, rows, columns, gate, up):
    half, inner = gate.shape
    pieces = (n, half // n, inner)
    shape = jax.ShapeDtypeStruct(pieces, gate.dtype)
    everywhere, vmem = pl.BlockSpec(memory_space=pl.ANY), pl.BlockSpec(memory_space=pltpu.VMEM)
    return pl.pallas_call(
        functools.partial(move_kernel, n, factor),
        out_shape=(shape, shape),
        in_specs=[pl.BlockSpec(memory_space=pltpu.SMEM), vmem, vmem, vmem, everywhere, everywhere],
        out_specs=(everywhere, everywhere),
        scratch_shapes=[
            pltpu.VMEM((2, half, inner), gate.dtype),
            pltpu.VMEM((2,) + rows.shape, rows.dtype),
        ]
        + [pltpu.VMEM(pieces, gate.dtype)] * 6
        + [
            pltpu.SemaphoreType.DMA((2,)),
            pltpu.SemaphoreType.DMA((4,)),
            pltpu.SemaphoreType.DMA((4,)),
            pltpu.SemaphoreType.DMA((4,)),
            pltpu.SemaphoreType.DMA((2,)),
        ],
        compiler_params=pltpu.CompilerParams(
            collective_id=2, has_side_effects=True, vmem_limit_bytes=48 * 2**20
        ),
        name="move",
    )(inverse, kernel_matrix, rows, columns, gate, up)


def shards(
    dy,
    probs,
    expert_ids,
    copy_choice,
    saved_inputs,
    saved_gate,
    saved_up,
    down_weight,
    gate_weight,
    up_weight,
    new_owner,
):
    copy_index = lax.axis_index("rep")
    experts = lax.axis_size("ep")
    capacity = saved_inputs.shape[3]
    tokens, width = dy.shape
    inner = saved_gate.shape[4]
    half = width // 2
    first = copy_index == 0

    expert = jnp.arange(experts, dtype=jnp.int32)
    hits = (expert_ids[:, :, None] == expert) & (copy_choice == copy_index)[:, :, None]
    chosen = jnp.any(hits, axis=1)
    weight = jnp.sum(jnp.where(hits, probs[:, :, None], 0.0), axis=1)
    before = jnp.tril(jnp.ones((tokens, tokens), jnp.bfloat16), -1)
    position = jnp.dot(before, chosen.astype(jnp.bfloat16), preferred_element_type=jnp.float32)
    slot = jnp.arange(capacity, dtype=jnp.float32)
    select = chosen[:, :, None] & (position[:, :, None] == slot)
    scale = jnp.sum(jnp.where(select, weight[:, :, None], 0.0), axis=0)
    rows = lax.dot_general(
        select.astype(jnp.bfloat16), dy, (((0,), (0,)), ((), ())), preferred_element_type=jnp.float32
    )
    outgoing = (scale[:, :, None] * rows).astype(jnp.bfloat16)
    routed = exchange(outgoing).reshape(experts * capacity, width)

    def ordered(own, other, axis):
        return jnp.where(first, jnp.concatenate([own, other], axis), jnp.concatenate([other, own], axis))

    down = down_weight[0]
    hidden_grad = dot(routed, ordered(down, from_partner(down), 1), ((1,), (1,))) / math.sqrt(inner)
    gate_value = saved_gate.reshape(-1, inner).astype(jnp.float32)
    up_value = saved_up.reshape(-1, inner).astype(jnp.float32)
    sigmoid = jax.nn.sigmoid(gate_value)
    gate_rows = (hidden_grad * up_value * sigmoid * (1.0 + gate_value * (1.0 - sigmoid))).astype(jnp.bfloat16)
    up_rows = (hidden_grad * gate_value * sigmoid).astype(jnp.bfloat16)
    own_rows = jnp.where(first, gate_rows, up_rows)
    other_rows = from_partner(jnp.where(first, up_rows, gate_rows))
    factor_rows = ordered(own_rows, other_rows, 0)

    inputs = saved_inputs.reshape(-1, width)
    all_inputs = ordered(inputs, from_partner(inputs), 0)
    kernel_matrix = dot(all_inputs, all_inputs, ((1,), (1,)))
    columns = jnp.where(first, all_inputs[:, :half], all_inputs[:, half:])
    inverse = jnp.sum(
        jnp.where(new_owner[:, None] == expert[None, :], expert[:, None], 0), axis=0, dtype=jnp.int32
    )
    own, other = move(
        experts, step_scale * math.sqrt(width), inverse, kernel_matrix, factor_rows, columns, gate_weight[0], up_weight[0]
    )
    new_gate, new_up = jnp.where(first, own, other), jnp.where(first, other, own)
    return new_gate.reshape(1, half, inner), new_up.reshape(1, half, inner)


def solution(mesh):
    in_specs = (
        P("ep", None),
        P("ep", None),
        P("ep", None),
        P("ep", None),
        P("ep", "rep", None, None, None),
        P("ep", "rep", None, None, None),
        P("ep", "rep", None, None, None),
        P("ep", None, "rep"),
        P("ep", "rep", None),
        P("ep", "rep", None),
        P(),
    )
    out_specs = (P("ep", "rep", None), P("ep", "rep", None))
    return jax.shard_map(shards, mesh=mesh, in_specs=in_specs, out_specs=out_specs, check_vma=False)
```

```python
import functools
import math

import jax
import jax.numpy as jnp
from jax import lax
from jax.experimental import pallas as pl
from jax.experimental.pallas import tpu as pltpu
from jax.sharding import PartitionSpec as P

MESH = pl.DeviceIdType.MESH
ITERS = 2

quintic_first = 3.4445
quintic_second = -4.775
quintic_third = 2.0315
step_scale = 2.0
epsilon = 1e-07

GRID = (4, 4, 8)


def shifted(me, k):
    ny, nx, nz = GRID
    y, x, z = me // (nx * nz), (me // nz) % nx, me % nz
    dy, dx, dz = k // (nx * nz), (k // nz) % nx, k % nz
    return (lax.rem(y + dy, ny) * nx + lax.rem(x + dx, nx)) * nz + lax.rem(z + dz, nz)


def dot(a, b, dims):
    return lax.dot_general(a, b, (dims, ((), ())), preferred_element_type=jnp.float32)


CHUNKS = 2


def shift_of(size):
    assert size & (size - 1) == 0
    return size.bit_length() - 1


def selection(key_columns, plane, top, sources, tokens, spots, capacity):
    count = sources * tokens
    lanes = 2 * spots * sources * capacity
    lane = lax.broadcasted_iota(jnp.int32, (1, lanes), 1)
    slot = lane & (capacity - 1)
    source = (lane >> shift_of(capacity)) & (sources - 1)
    spot = (lane >> shift_of(capacity * sources)) & (spots - 1)
    copy = lane >> shift_of(capacity * sources * spots)
    wanted = (((spot * sources + plane) * 2) + copy).astype(jnp.float32)
    here = (lax.broadcasted_iota(jnp.int32, (count, 1), 0) >> shift_of(tokens)) == source
    taken = jnp.zeros((count, lanes), jnp.float32)
    weight = jnp.zeros((count, lanes), jnp.float32)
    for k in range(top):
        hit = (key_columns[:, k : k + 1] == wanted) & here
        taken = jnp.where(hit, 1.0, taken)
        weight = jnp.where(hit, key_columns[:, top + k : top + k + 1], weight)
    row = lax.broadcasted_iota(jnp.int32, (count, count), 0)
    column = lax.broadcasted_iota(jnp.int32, (count, count), 1)
    before = jnp.where(row > column, 1.0, 0.0).astype(jnp.bfloat16)
    position = dot(before, taken.astype(jnp.bfloat16), ((1,), (0,)))
    mine = (taken > 0.5) & (position == slot.astype(jnp.float32))
    ones = jnp.ones((count, 128), jnp.bfloat16)
    left = jnp.where(mine, weight, 0.0)
    scale = None
    for _ in range(3):
        part = left.astype(jnp.bfloat16)
        left = left - part.astype(jnp.float32)
        term = dot(part, ones, ((0,), (0,)))
        scale = term if scale is None else scale + term
    return jnp.where(mine, 1.0, 0.0).astype(jnp.bfloat16), scale


def remote(src, dst, send, recv, to):
    return pltpu.make_async_remote_copy(
        src_ref=src, dst_ref=dst, send_sem=send, recv_sem=recv, device_id=to, device_id_type=MESH
    )


def route_kernel(
    top, meta_ref, dy_ref, x_ref, g_ref, u_ref, down_ref, k_out, r_out, x_out,
    line, keys, sent, routed, inputs, down, rows, other,
    line_send, line_recv, keys_sem, plane_send, plane_recv, near_send, near_recv, pair_send, pair_recv,
    own_sem, piece_sem,
):
    me = lax.axis_index("ep")
    core = lax.axis_index("rep")
    nz = GRID[2]
    spots = GRID[0] * GRID[1]
    z, spot = me % nz, me // nz
    tokens, width = line.shape[2], line.shape[3]
    capacity = sent.shape[3] // nz
    half = CHUNKS * width
    partner = {"rep": 1 - core}

    def above(k):
        return {"ep": shifted(me, k)}

    barrier = pltpu.get_barrier_semaphore()

    def greet_line(k, carry):
        pl.semaphore_signal(barrier, inc=1, device_id=above(k), device_id_type=MESH)
        return carry

    def greet_plane(k, carry):
        for c in range(2):
            pl.semaphore_signal(
                barrier, inc=1, device_id={"ep": shifted(me, k * nz), "rep": c}, device_id_type=MESH
            )
        return carry

    lax.fori_loop(1, nz, greet_line, 0)
    lax.fori_loop(1, spots, greet_plane, 0)
    pl.semaphore_signal(barrier, inc=1, device_id=partner, device_id_type=MESH)

    def columns(chunk):
        return pl.ds(pl.multiple_of(core * half + chunk * width, width), width)

    own = [pltpu.make_async_copy(dy_ref.at[:, columns(h)], line.at[h, z], own_sem.at[h]) for h in range(CHUNKS)]
    own.append(pltpu.make_async_copy(meta_ref, keys.at[z], own_sem.at[CHUNKS]))
    own.append(pltpu.make_async_copy(x_ref, inputs.at[core], own_sem.at[CHUNKS + 1]))
    own.append(pltpu.make_async_copy(down_ref, down.at[core], own_sem.at[CHUNKS + 2]))
    for copy in own:
        copy.start()
    pl.semaphore_wait(barrier, nz + 2 * (spots - 1))

    def send_keys(k, carry):
        remote(meta_ref, keys.at[z], keys_sem.at[0], keys_sem.at[1], above(k)).start()
        return carry

    lax.fori_loop(1, nz, send_keys, 0)
    for h in range(CHUNKS):

        def send_line(k, carry, h=h):
            remote(dy_ref.at[:, columns(h)], line.at[h, z], line_send.at[h], line_recv.at[h], above(k)).start()
            return carry

        lax.fori_loop(1, nz, send_line, 0)
    swaps = [
        remote(x_ref, inputs.at[core], pair_send.at[0], pair_recv.at[0], partner),
        remote(down_ref, down.at[core], pair_send.at[1], pair_recv.at[1], partner),
    ]
    for swap in swaps:
        swap.start()

    others = pl.ds(0, nz - 1)
    all_keys = remote(keys.at[others], keys.at[others], keys_sem.at[0], keys_sem.at[1], above(1))
    all_keys.wait_recv()
    own[CHUNKS].wait()
    choose, scale = selection(
        keys[...].reshape(nz * tokens, keys.shape[2]), z, top, nz, tokens, spots, capacity
    )
    scale = jnp.concatenate([scale] * (width // scale.shape[1]), axis=1)
    for h in range(CHUNKS):
        own[h].wait()
        remote(line.at[h, others], line.at[h, others], line_send.at[h], line_recv.at[h], above(1)).wait_recv()
        picked = dot(choose, line[h].reshape(nz * tokens, width), ((0,), (0,)))
        sent[h] = (picked * scale).astype(jnp.bfloat16).reshape(sent.shape[1:])

        def send_plane(k, carry, h=h):
            to = shifted(me, k * nz)
            for c in range(2):
                remote(
                    sent.at[h, c, to // nz], routed.at[spot, :, columns(h)],
                    plane_send.at[h], plane_recv.at[h], {"ep": to, "rep": c},
                ).start()
            return carry

        lax.fori_loop(1, spots, send_plane, 0)
        remote(
            sent.at[h, 1 - core, spot], routed.at[spot, :, columns(h)], near_send.at[h], near_recv.at[h], partner
        ).start()
        pltpu.make_async_copy(
            sent.at[h, core, spot], routed.at[spot, :, columns(h)], piece_sem.at[h]
        ).start()

    own[CHUNKS + 1].wait()
    swaps[0].wait_recv()
    copies, pairs, features = inputs.shape
    everything = inputs[...].reshape(copies * pairs, features)
    k_out[...] = dot(everything, everything, ((1,), (1,)))
    for c in range(2):
        x_out[c] = inputs[c, :, pl.ds(pl.multiple_of(core * half, half), half)]
    gate_value = g_ref[...].astype(jnp.float32).reshape(pairs, g_ref.shape[-1])
    up_value = u_ref[...].astype(jnp.float32).reshape(pairs, u_ref.shape[-1])
    own[CHUNKS + 2].wait()
    swaps[1].wait_recv()
    near = pl.ds(0, spots - 1)
    for h in range(CHUNKS):
        pltpu.make_async_copy(sent.at[h, core, spot], routed.at[spot, :, columns(h)], piece_sem.at[h]).wait()
        remote(
            sent.at[h, 1 - core, spot], routed.at[spot, :, columns(h)], near_send.at[h], near_recv.at[h], partner
        ).wait_recv()
        both = routed.at[near, :, pl.ds(h * 2 * width, 2 * width)]
        remote(both, both, plane_send.at[h], plane_recv.at[h], partner).wait_recv()

    arrived = routed[...].reshape(pairs, features)
    hidden = dot(arrived[:, :half], down[0], ((1,), (1,))) + dot(arrived[:, half:], down[1], ((1,), (1,)))
    hidden = hidden / math.sqrt(hidden.shape[1])
    sigmoid = jax.nn.sigmoid(gate_value)
    gate_rows = hidden * up_value * sigmoid * (1.0 + gate_value * (1.0 - sigmoid))
    up_rows = hidden * gate_value * sigmoid
    first = core == 0
    rows[core] = jnp.where(first, gate_rows, up_rows).astype(jnp.bfloat16)
    other[...] = jnp.where(first, up_rows, gate_rows).astype(jnp.bfloat16)
    last = remote(other, rows.at[core], pair_send.at[2], pair_recv.at[2], partner)
    last.start()

    all_keys.wait_send()
    for swap in swaps:
        swap.wait_send()
    for h in range(CHUNKS):
        remote(line.at[h, others], line.at[h, others], line_send.at[h], line_recv.at[h], above(1)).wait_send()
        remote(
            sent.at[h, 1 - core, spot], routed.at[spot, :, columns(h)], near_send.at[h], near_recv.at[h], partner
        ).wait_send()
        both = sent.at[h, :, near]
        remote(both, both, plane_send.at[h], plane_recv.at[h], partner).wait_send()
    last.wait_send()
    last.wait_recv()
    r_out[...] = rows[...]


def route(meta, dy, inputs, gate, up, down, top):
    pairs, features = inputs.shape
    inner, half = down.shape
    tokens = dy.shape[0]
    nz, spots = GRID[2], GRID[0] * GRID[1]
    slots = pairs // spots
    width = half // CHUNKS
    everywhere, vmem = pl.BlockSpec(memory_space=pl.ANY), pl.BlockSpec(memory_space=pltpu.VMEM)
    bf16 = jnp.bfloat16
    semaphores = pltpu.SemaphoreType.DMA
    return pl.pallas_call(
        functools.partial(route_kernel, top),
        out_shape=(
            jax.ShapeDtypeStruct((2 * pairs, 2 * pairs), jnp.float32),
            jax.ShapeDtypeStruct((2, pairs, inner), bf16),
            jax.ShapeDtypeStruct((2, pairs, half), bf16),
        ),
        in_specs=[everywhere, everywhere, everywhere, vmem, vmem, everywhere],
        out_specs=(vmem, vmem, vmem),
        scratch_shapes=[
            pltpu.VMEM((CHUNKS, nz, tokens, width), bf16),
            pltpu.VMEM((nz,) + meta.shape, jnp.float32),
            pltpu.VMEM((CHUNKS, 2, spots, slots, width), bf16),
            pltpu.VMEM((spots, slots, features), bf16),
            pltpu.VMEM((2, pairs, features), bf16),
            pltpu.VMEM((2, inner, half), bf16),
            pltpu.VMEM((2, pairs, inner), bf16),
            pltpu.VMEM((pairs, inner), bf16),
            semaphores((CHUNKS,)),
            semaphores((CHUNKS,)),
            semaphores((2,)),
            semaphores((CHUNKS,)),
            semaphores((CHUNKS,)),
            semaphores((CHUNKS,)),
            semaphores((CHUNKS,)),
            semaphores((3,)),
            semaphores((3,)),
            semaphores((CHUNKS + 3,)),
            semaphores((CHUNKS,)),
        ],
        compiler_params=pltpu.CompilerParams(
            collective_id=1, has_side_effects=True, vmem_limit_bytes=48 * 2**20
        ),
        name="route",
    )(meta, dy, inputs, gate, up, down)


def orthogonal_factor(kernel_matrix, rows):
    high = kernel_matrix.astype(jnp.bfloat16)
    low = (kernel_matrix - high.astype(jnp.float32)).astype(jnp.bfloat16)
    product = dot(high, rows, ((1,), (0,))) + dot(low, rows, ((1,), (0,)))
    total = jnp.sqrt(jnp.maximum(jnp.sum(rows.astype(jnp.float32) * product), 0.0))
    scale = 1.0 / (total + epsilon)
    product = product * (scale * scale)
    for repeat in range(ITERS):
        if repeat:
            product = dot(high, rows, ((1,), (0,))) + dot(low, rows, ((1,), (0,)))
        gram = dot(rows, product.astype(jnp.bfloat16), ((0,), (0,)))
        half = gram.astype(jnp.bfloat16)
        square = dot(half, half, ((1,), (0,)))
        poly = (quintic_second * gram + quintic_third * square).astype(jnp.bfloat16)
        mixed = quintic_first * rows.astype(jnp.float32) + dot(rows, poly, ((1,), (0,)))
        if not repeat:
            mixed = mixed * scale
        rows = mixed.astype(jnp.bfloat16)
    return rows


def move_kernel(
    n, factor, inverse, k_ref, r_ref, x_ref, gate_ref, up_ref, own_out, other_out,
    weights, factors, made0, made1, held0, held1, ready0, ready1, load, send, recv, local, swap,
):
    me = lax.axis_index("ep")
    core = lax.axis_index("rep")
    outs, made, held, ready = (own_out, other_out), (made0, made1), (held0, held1), (ready0, ready1)
    ny = GRID[0]
    group = n // ny
    piece = weights.shape[1] // n
    block = group * piece
    rest = pl.ds(0, n - 1)
    partner = {"rep": 1 - core}

    barrier = pltpu.get_barrier_semaphore()

    def say(k, carry):
        pl.semaphore_signal(barrier, inc=1, device_id={"ep": shifted(me, k)}, device_id_type=MESH)
        return carry

    lax.fori_loop(1, n, say, 0)
    pl.semaphore_signal(barrier, inc=1, device_id=partner, device_id_type=MESH)

    for c, refs in enumerate(((gate_ref, up_ref), (up_ref, gate_ref))):
        @pl.when(core == c)
        def _(refs=refs):
            for q in range(2):
                pltpu.make_async_copy(refs[q], weights.at[q], load.at[q]).start()

    factors[0] = orthogonal_factor(k_ref[...], r_ref[...])
    pl.semaphore_wait(barrier, n)
    trade = pltpu.make_async_remote_copy(
        src_ref=factors.at[0], dst_ref=factors.at[1], send_sem=swap.at[0], recv_sem=swap.at[1],
        device_id=partner, device_id_type=MESH,
    )
    trade.start()

    for q in range(2):
        pltpu.make_async_copy(gate_ref, weights.at[q], load.at[q]).wait()
        if q:
            trade.wait_recv()

        def spread(k, carry, q=q):
            to = shifted(me, k)
            pltpu.make_async_remote_copy(
                src_ref=made[q].at[to], dst_ref=held[q].at[me], send_sem=send.at[q], recv_sem=recv.at[q],
                device_id={"ep": to}, device_id_type=MESH,
            ).start()
            return carry

        def produce(dy, carry, q=q):
            y = lax.rem(me // group + dy, ny)
            rows = pl.ds(pl.multiple_of(y * block, block), block)
            ortho = dot(x_ref[:, rows], factors[q], ((0,), (0,)))
            fresh = (weights[q, rows, :].astype(jnp.float32) - factor * ortho).astype(jnp.bfloat16)
            made[q][pl.ds(y * group, group)] = fresh.reshape(group, piece, fresh.shape[1])
            lax.fori_loop(jnp.where(dy == 0, 1, dy * group), (dy + 1) * group, spread, 0)
            return carry

        lax.fori_loop(0, ny, produce, 0)
        pltpu.make_async_copy(made[q].at[me], held[q].at[me], local.at[q]).start()

    for q in range(2):
        pltpu.make_async_copy(made[q].at[me], held[q].at[me], local.at[q]).wait()
        pltpu.make_async_remote_copy(
            src_ref=made[q].at[rest], dst_ref=held[q].at[rest], send_sem=send.at[q], recv_sem=recv.at[q],
            device_id={"ep": shifted(me, 1)}, device_id_type=MESH,
        ).wait_recv()

        def collect(k, carry, q=q):
            to = shifted(me, k)
            ready[q][k] = held[q][inverse[to]]
            pltpu.make_async_remote_copy(
                src_ref=ready[q].at[k], dst_ref=outs[q].at[me], send_sem=send.at[2 + q], recv_sem=recv.at[2 + q],
                device_id={"ep": to}, device_id_type=MESH,
            ).start()
            return carry

        lax.fori_loop(1, n, collect, 0)
        ready[q][0] = held[q][inverse[me]]
        pltpu.make_async_copy(ready[q].at[0], outs[q].at[me], local.at[2 + q]).start()

    trade.wait_send()
    for q in range(2):
        pltpu.make_async_copy(ready[q].at[0], outs[q].at[me], local.at[2 + q]).wait()
        pltpu.make_async_remote_copy(
            src_ref=made[q].at[rest], dst_ref=held[q].at[rest], send_sem=send.at[q], recv_sem=recv.at[q],
            device_id={"ep": shifted(me, 1)}, device_id_type=MESH,
        ).wait_send()
        last = pltpu.make_async_remote_copy(
            src_ref=ready[q].at[rest], dst_ref=outs[q].at[rest], send_sem=send.at[2 + q], recv_sem=recv.at[2 + q],
            device_id={"ep": shifted(me, 1)}, device_id_type=MESH,
        )
        last.wait_send()
        last.wait_recv()


def move(n, factor, inverse, kernel_matrix, rows, columns, gate, up):
    half, inner = gate.shape
    pieces = (n, half // n, inner)
    shape = jax.ShapeDtypeStruct(pieces, gate.dtype)
    everywhere, vmem = pl.BlockSpec(memory_space=pl.ANY), pl.BlockSpec(memory_space=pltpu.VMEM)
    return pl.pallas_call(
        functools.partial(move_kernel, n, factor),
        out_shape=(shape, shape),
        in_specs=[pl.BlockSpec(memory_space=pltpu.SMEM), vmem, vmem, vmem, everywhere, everywhere],
        out_specs=(everywhere, everywhere),
        scratch_shapes=[
            pltpu.VMEM((2, half, inner), gate.dtype),
            pltpu.VMEM((2,) + rows.shape, rows.dtype),
        ]
        + [pltpu.VMEM(pieces, gate.dtype)] * 6
        + [
            pltpu.SemaphoreType.DMA((2,)),
            pltpu.SemaphoreType.DMA((4,)),
            pltpu.SemaphoreType.DMA((4,)),
            pltpu.SemaphoreType.DMA((4,)),
            pltpu.SemaphoreType.DMA((2,)),
        ],
        compiler_params=pltpu.CompilerParams(
            collective_id=2, has_side_effects=True, vmem_limit_bytes=48 * 2**20
        ),
        name="move",
    )(inverse, kernel_matrix, rows, columns, gate, up)


def shards(
    dy,
    probs,
    expert_ids,
    copy_choice,
    saved_inputs,
    saved_gate,
    saved_up,
    down_weight,
    gate_weight,
    up_weight,
    new_owner,
):
    first = lax.axis_index("rep") == 0
    experts = lax.axis_size("ep")
    tokens, width = dy.shape
    top = expert_ids.shape[1]
    inner = saved_gate.shape[4]
    half = width // 2
    keyed = (expert_ids * 2 + copy_choice).astype(jnp.float32)
    meta = jnp.concatenate([keyed, probs, jnp.zeros((tokens, 128 - 2 * top), jnp.float32)], axis=1)
    kernel_matrix, rows, columns = route(
        meta, dy, saved_inputs.reshape(-1, width), saved_gate[0, 0], saved_up[0, 0], down_weight[0], top
    )
    factor_rows, columns = rows.reshape(-1, inner), columns.reshape(-1, half)
    expert = jnp.arange(experts, dtype=jnp.int32)
    inverse = jnp.sum(
        jnp.where(new_owner[:, None] == expert[None, :], expert[:, None], 0), axis=0, dtype=jnp.int32
    )
    own, other = move(
        experts, step_scale * math.sqrt(width), inverse, kernel_matrix, factor_rows, columns, gate_weight[0], up_weight[0]
    )
    new_gate, new_up = jnp.where(first, own, other), jnp.where(first, other, own)
    return new_gate.reshape(1, half, inner), new_up.reshape(1, half, inner)


def solution(mesh):
    in_specs = (
        P("ep", None),
        P("ep", None),
        P("ep", None),
        P("ep", None),
        P("ep", "rep", None, None, None),
        P("ep", "rep", None, None, None),
        P("ep", "rep", None, None, None),
        P("ep", None, "rep"),
        P("ep", "rep", None),
        P("ep", "rep", None),
        P(),
    )
    out_specs = (P("ep", "rep", None), P("ep", "rep", None))
    return jax.shard_map(shards, mesh=mesh, in_specs=in_specs, out_specs=out_specs, check_vma=False)
```

```python
import functools
import math

import jax
import jax.numpy as jnp
from jax import lax
from jax.experimental import pallas as pl
from jax.experimental.pallas import tpu as pltpu
from jax.sharding import PartitionSpec as P

MESH = pl.DeviceIdType.MESH
ITERS = 2

quintic_first = 3.4445
quintic_second = -4.775
quintic_third = 2.0315
step_scale = 2.0
epsilon = 1e-07

GRID = (4, 4, 8)


def shifted(me, k):
    ny, nx, nz = GRID
    y, x, z = me // (nx * nz), (me // nz) % nx, me % nz
    dy, dx, dz = k // (nx * nz), (k // nz) % nx, k % nz
    return (lax.rem(y + dy, ny) * nx + lax.rem(x + dx, nx)) * nz + lax.rem(z + dz, nz)


def dot(a, b, dims):
    return lax.dot_general(a, b, (dims, ((), ())), preferred_element_type=jnp.float32)


CHUNKS = 4


def shift_of(size):
    assert size & (size - 1) == 0
    return size.bit_length() - 1


def selection(table, plane, top, sources, tokens, spots, capacity):
    count = sources * tokens
    lanes = 2 * spots * sources * capacity
    lane = lax.broadcasted_iota(jnp.int32, (1, lanes), 1)
    slot = lane & (capacity - 1)
    source = (lane >> shift_of(capacity)) & (sources - 1)
    spot = (lane >> shift_of(capacity * sources)) & (spots - 1)
    copy = lane >> shift_of(capacity * sources * spots)
    wanted = (((spot * sources + plane) * 2) + copy).astype(jnp.float32)
    blocks, weights = [], []
    for z in range(sources):
        aim = jnp.where(source == z, wanted, -1.0)
        block = jnp.zeros((tokens, lanes), jnp.float32)
        weight = jnp.zeros((tokens, lanes), jnp.float32)
        for k in range(top):
            at = z * 2 * top + k
            hit = table[:, at : at + 1] == aim
            block = jnp.where(hit, 1.0, block)
            weight = jnp.where(hit, table[:, at + top : at + top + 1], weight)
        blocks.append(block)
        weights.append(weight)
    taken = jnp.concatenate(blocks, axis=0)
    weight = jnp.concatenate(weights, axis=0)
    row = lax.broadcasted_iota(jnp.int32, (count, count), 0)
    column = lax.broadcasted_iota(jnp.int32, (count, count), 1)
    before = jnp.where(row > column, 1.0, 0.0).astype(jnp.bfloat16)
    position = dot(before, taken.astype(jnp.bfloat16), ((1,), (0,)))
    mine = (taken > 0.5) & (position == slot.astype(jnp.float32))
    ones = jnp.ones((count, 128), jnp.bfloat16)
    left = jnp.where(mine, weight, 0.0)
    scale = None
    for _ in range(3):
        part = left.astype(jnp.bfloat16)
        left = left - part.astype(jnp.float32)
        term = dot(part, ones, ((0,), (0,)))
        scale = term if scale is None else scale + term
    return jnp.where(mine, 1.0, 0.0).astype(jnp.bfloat16), scale


def remote(src, dst, send, recv, to):
    return pltpu.make_async_remote_copy(
        src_ref=src, dst_ref=dst, send_sem=send, recv_sem=recv, device_id=to, device_id_type=MESH
    )


def route_kernel(
    top, ids_ref, copy_ref, probs_ref, owner_ref, dy_ref, x_ref, g_ref, u_ref, down_ref, k_out, r_out, x_out, inverse_out,
    line, meta, gates, keys, sent, routed, raw, inputs, down, rows, other,
    line_send, line_recv, keys_sem, plane_send, plane_recv, near_send, near_recv, pair_send, pair_recv,
    own_sem, piece_sem,
):
    me = lax.axis_index("ep")
    core = lax.axis_index("rep")
    nz = GRID[2]
    spots = GRID[0] * GRID[1]
    z, spot = me % nz, me // nz
    tokens, width = line.shape[2], line.shape[3]
    capacity = sent.shape[3] // nz
    half = CHUNKS * width
    partner = {"rep": 1 - core}

    def above(k):
        return {"ep": shifted(me, k)}

    count = ids_ref.shape[1]
    keyed = (ids_ref[...] * 2 + copy_ref[...]).astype(jnp.float32)
    packed = jnp.concatenate([keyed, probs_ref[...]], axis=0)
    meta[...] = jnp.concatenate([packed, jnp.zeros((2 * top, 128 - count), jnp.float32)], axis=1)
    barrier = pltpu.get_barrier_semaphore()

    def greet_line(k, carry):
        pl.semaphore_signal(barrier, inc=1, device_id=above(k), device_id_type=MESH)
        return carry

    def greet_plane(k, carry):
        for c in range(2):
            pl.semaphore_signal(
                barrier, inc=1, device_id={"ep": shifted(me, k * nz), "rep": c}, device_id_type=MESH
            )
        return carry

    lax.fori_loop(1, nz, greet_line, 0)
    lax.fori_loop(1, spots, greet_plane, 0)
    pl.semaphore_signal(barrier, inc=1, device_id=partner, device_id_type=MESH)

    def columns(chunk):
        return pl.ds(pl.multiple_of(core * half + chunk * width, width), width)

    own = [pltpu.make_async_copy(dy_ref.at[:, columns(h)], line.at[h, z], own_sem.at[h]) for h in range(CHUNKS)]
    own.append(pltpu.make_async_copy(meta, keys.at[z], own_sem.at[CHUNKS]))
    own.append(pltpu.make_async_copy(x_ref, raw.at[core], own_sem.at[CHUNKS + 1]))
    own.append(pltpu.make_async_copy(down_ref, down.at[core], own_sem.at[CHUNKS + 2]))
    own.append(pltpu.make_async_copy(g_ref, gates.at[0], own_sem.at[CHUNKS + 3]))
    own.append(pltpu.make_async_copy(u_ref, gates.at[1], own_sem.at[CHUNKS + 4]))
    for copy in own:
        copy.start()
    pl.semaphore_wait(barrier, nz + 2 * (spots - 1))

    def send_keys(k, carry):
        remote(meta, keys.at[z], keys_sem.at[0], keys_sem.at[1], above(k)).start()
        return carry

    lax.fori_loop(1, nz, send_keys, 0)
    for h in range(CHUNKS):

        def send_line(k, carry, h=h):
            remote(dy_ref.at[:, columns(h)], line.at[h, z], line_send.at[h], line_recv.at[h], above(k)).start()
            return carry

        lax.fori_loop(1, nz, send_line, 0)
    swaps = [
        remote(x_ref, raw.at[core], pair_send.at[0], pair_recv.at[0], partner),
        remote(down_ref, down.at[core], pair_send.at[1], pair_recv.at[1], partner),
    ]
    for swap in swaps:
        swap.start()

    others = pl.ds(0, nz - 1)
    all_keys = remote(keys.at[others], keys.at[others], keys_sem.at[0], keys_sem.at[1], above(1))
    all_keys.wait_recv()
    own[CHUNKS].wait()
    table = keys[...].reshape(nz * 2 * top, 128).T
    choose, scale = selection(
        table[:count], z, top, nz, tokens, spots, capacity
    )
    scale = jnp.concatenate([scale] * (width // scale.shape[1]), axis=1)
    for h in range(CHUNKS):
        own[h].wait()
        remote(line.at[h, others], line.at[h, others], line_send.at[h], line_recv.at[h], above(1)).wait_recv()
        picked = dot(choose, line[h].reshape(nz * tokens, width), ((0,), (0,)))
        sent[h] = (picked * scale).astype(jnp.bfloat16).reshape(sent.shape[1:])

        def send_plane(k, carry, h=h):
            to = shifted(me, k * nz)
            for c in range(2):
                remote(
                    sent.at[h, c, to // nz], routed.at[spot, :, columns(h)],
                    plane_send.at[h], plane_recv.at[h], {"ep": to, "rep": c},
                ).start()
            return carry

        lax.fori_loop(1, spots, send_plane, 0)
        remote(
            sent.at[h, 1 - core, spot], routed.at[spot, :, columns(h)], near_send.at[h], near_recv.at[h], partner
        ).start()
        pltpu.make_async_copy(
            sent.at[h, core, spot], routed.at[spot, :, columns(h)], piece_sem.at[h]
        ).start()

    own[CHUNKS + 1].wait()
    swaps[0].wait_recv()
    copies, pairs, features = inputs.shape
    for c in range(2):
        inputs[c] = raw[c].astype(jnp.float32).reshape(pairs, features).astype(jnp.bfloat16)
    everything = inputs[...].reshape(copies * pairs, features)
    k_out[...] = dot(everything, everything, ((1,), (1,)))
    for c in range(2):
        x_out[c] = inputs[c, :, pl.ds(pl.multiple_of(core * half, half), half)]
    own[CHUNKS + 3].wait()
    own[CHUNKS + 4].wait()
    gate_value = gates[0].astype(jnp.float32).reshape(pairs, g_ref.shape[-1])
    up_value = gates[1].astype(jnp.float32).reshape(pairs, u_ref.shape[-1])
    experts = owner_ref.shape[1]
    low = lax.broadcasted_iota(jnp.int32, (experts, experts), 0)
    wide = lax.broadcasted_iota(jnp.int32, (experts, experts), 1).astype(jnp.float32)
    held = jnp.sum(jnp.where(owner_ref[...] == low, wide, 0.0), axis=1, keepdims=True)
    inverse_out[...] = jnp.broadcast_to(held, (experts, experts)).T[:1].astype(jnp.int32)
    own[CHUNKS + 2].wait()
    swaps[1].wait_recv()
    near = pl.ds(0, spots - 1)
    hidden = None
    for h in range(CHUNKS):
        pltpu.make_async_copy(sent.at[h, core, spot], routed.at[spot, :, columns(h)], piece_sem.at[h]).wait()
        remote(
            sent.at[h, 1 - core, spot], routed.at[spot, :, columns(h)], near_send.at[h], near_recv.at[h], partner
        ).wait_recv()
        both = sent.at[h, :, near]
        remote(both, both, plane_send.at[h], plane_recv.at[h], partner).wait_recv()
        for c in range(2):
            here = routed[:, :, pl.ds(c * half + h * width, width)].reshape(pairs, width)
            term = dot(here, down[c, :, pl.ds(h * width, width)], ((1,), (1,)))
            hidden = term if hidden is None else hidden + term
    hidden = hidden / math.sqrt(hidden.shape[1])
    sigmoid = jax.nn.sigmoid(gate_value)
    gate_rows = hidden * up_value * sigmoid * (1.0 + gate_value * (1.0 - sigmoid))
    up_rows = hidden * gate_value * sigmoid
    first = core == 0
    rows[core] = jnp.where(first, gate_rows, up_rows).astype(jnp.bfloat16)
    other[...] = jnp.where(first, up_rows, gate_rows).astype(jnp.bfloat16)
    last = remote(other, rows.at[core], pair_send.at[2], pair_recv.at[2], partner)
    last.start()

    all_keys.wait_send()
    for swap in swaps:
        swap.wait_send()
    for h in range(CHUNKS):
        remote(line.at[h, others], line.at[h, others], line_send.at[h], line_recv.at[h], above(1)).wait_send()
        remote(
            sent.at[h, 1 - core, spot], routed.at[spot, :, columns(h)], near_send.at[h], near_recv.at[h], partner
        ).wait_send()
        both = sent.at[h, :, near]
        remote(both, both, plane_send.at[h], plane_recv.at[h], partner).wait_send()
    last.wait_send()
    last.wait_recv()
    r_out[...] = rows[...]


def route(ids, copies, probs, owner, dy, inputs, gate, up, down):
    top = ids.shape[0]
    pairs, features = inputs.shape[0] * inputs.shape[1], inputs.shape[2]
    inner, half = down.shape
    tokens = dy.shape[0]
    nz, spots = GRID[2], GRID[0] * GRID[1]
    slots = pairs // spots
    width = half // CHUNKS
    everywhere, vmem = pl.BlockSpec(memory_space=pltpu.HBM), pl.BlockSpec(memory_space=pltpu.VMEM)
    bf16 = jnp.bfloat16
    semaphores = pltpu.SemaphoreType.DMA
    return pl.pallas_call(
        functools.partial(route_kernel, top),
        out_shape=(
            jax.ShapeDtypeStruct((2 * pairs, 2 * pairs), jnp.float32),
            jax.ShapeDtypeStruct((2, pairs, inner), bf16),
            jax.ShapeDtypeStruct((2, pairs, half), bf16),
            jax.ShapeDtypeStruct(owner.shape, jnp.int32),
        ),
        in_specs=[vmem] * 4 + [everywhere] * 5,
        out_specs=(vmem, vmem, vmem, vmem),
        scratch_shapes=[
            pltpu.VMEM((CHUNKS, nz, tokens, width), bf16),
            pltpu.VMEM((2 * top, 128), jnp.float32),
            pltpu.VMEM((2,) + gate.shape, bf16),
            pltpu.VMEM((nz, 2 * top, 128), jnp.float32),
            pltpu.VMEM((CHUNKS, 2, spots, slots, width), bf16),
            pltpu.VMEM((spots, slots, features), bf16),
            pltpu.VMEM((2,) + inputs.shape, bf16),
            pltpu.VMEM((2, pairs, features), bf16),
            pltpu.VMEM((2, inner, half), bf16),
            pltpu.VMEM((2, pairs, inner), bf16),
            pltpu.VMEM((pairs, inner), bf16),
            semaphores((CHUNKS,)),
            semaphores((CHUNKS,)),
            semaphores((2,)),
            semaphores((CHUNKS,)),
            semaphores((CHUNKS,)),
            semaphores((CHUNKS,)),
            semaphores((CHUNKS,)),
            semaphores((3,)),
            semaphores((3,)),
            semaphores((CHUNKS + 5,)),
            semaphores((CHUNKS,)),
        ],
        compiler_params=pltpu.CompilerParams(
            collective_id=1, has_side_effects=True, vmem_limit_bytes=48 * 2**20
        ),
        name="route",
    )(ids, copies, probs, owner, dy, inputs, gate, up, down)


def orthogonal_factor(kernel_matrix, rows):
    high = kernel_matrix.astype(jnp.bfloat16)
    low = (kernel_matrix - high.astype(jnp.float32)).astype(jnp.bfloat16)
    scale = None
    for repeat in range(ITERS):
        square = dot(rows, rows, ((1,), (1,)))
        if not repeat:
            total = jnp.sqrt(jnp.maximum(jnp.sum(square * kernel_matrix), 0.0))
            scale = 1.0 / (total + epsilon)
            square = square * (scale * scale)
        square = square.astype(jnp.bfloat16)
        gram = dot(square, high, ((1,), (0,))) + dot(square, low, ((1,), (0,)))
        half = gram.astype(jnp.bfloat16)
        poly = quintic_second * gram + quintic_third * dot(half, half, ((1,), (0,)))
        mixed = quintic_first * rows.astype(jnp.float32) + dot(poly.astype(jnp.bfloat16), rows, ((1,), (0,)))
        if not repeat:
            mixed = mixed * scale
        rows = mixed.astype(jnp.bfloat16)
    return rows


def move_kernel(
    n, factor, inverse, k_ref, r_ref, x_ref, gate_ref, up_ref, own_out, other_out,
    weights, factors, made0, made1, held0, held1, ready0, ready1, load, send, recv, local, swap,
):
    me = lax.axis_index("ep")
    core = lax.axis_index("rep")
    outs, made, held, ready = (own_out, other_out), (made0, made1), (held0, held1), (ready0, ready1)
    ny = GRID[0]
    group = n // ny
    piece = weights.shape[1] // n
    block = group * piece
    rest = pl.ds(0, n - 1)
    partner = {"rep": 1 - core}

    barrier = pltpu.get_barrier_semaphore()

    def say(k, carry):
        pl.semaphore_signal(barrier, inc=1, device_id={"ep": shifted(me, k)}, device_id_type=MESH)
        return carry

    lax.fori_loop(1, n, say, 0)
    pl.semaphore_signal(barrier, inc=1, device_id=partner, device_id_type=MESH)

    for c, refs in enumerate(((gate_ref, up_ref), (up_ref, gate_ref))):
        @pl.when(core == c)
        def _(refs=refs):
            for q in range(2):
                pltpu.make_async_copy(refs[q], weights.at[q], load.at[q]).start()

    factors[0] = orthogonal_factor(k_ref[...], r_ref[...])
    pl.semaphore_wait(barrier, n)
    trade = pltpu.make_async_remote_copy(
        src_ref=factors.at[0], dst_ref=factors.at[1], send_sem=swap.at[0], recv_sem=swap.at[1],
        device_id=partner, device_id_type=MESH,
    )
    trade.start()

    for q in range(2):
        pltpu.make_async_copy(gate_ref, weights.at[q], load.at[q]).wait()
        if q:
            trade.wait_recv()

        def spread(k, carry, q=q):
            to = shifted(me, k)
            pltpu.make_async_remote_copy(
                src_ref=made[q].at[to], dst_ref=held[q].at[me], send_sem=send.at[q], recv_sem=recv.at[q],
                device_id={"ep": to}, device_id_type=MESH,
            ).start()
            return carry

        def produce(dy, carry, q=q):
            y = lax.rem(me // group + dy, ny)
            rows = pl.ds(pl.multiple_of(y * block, block), block)
            ortho = dot(x_ref[:, rows], factors[q], ((0,), (0,)))
            fresh = (weights[q, rows, :].astype(jnp.float32) - factor * ortho).astype(jnp.bfloat16)
            made[q][pl.ds(y * group, group)] = fresh.reshape(group, piece, fresh.shape[1])
            lax.fori_loop(jnp.where(dy == 0, 1, dy * group), (dy + 1) * group, spread, 0)
            return carry

        lax.fori_loop(0, ny, produce, 0)
        pltpu.make_async_copy(made[q].at[me], held[q].at[me], local.at[q]).start()

    for q in range(2):
        pltpu.make_async_copy(made[q].at[me], held[q].at[me], local.at[q]).wait()
        pltpu.make_async_remote_copy(
            src_ref=made[q].at[rest], dst_ref=held[q].at[rest], send_sem=send.at[q], recv_sem=recv.at[q],
            device_id={"ep": shifted(me, 1)}, device_id_type=MESH,
        ).wait_recv()

        def collect(k, carry, q=q):
            to = shifted(me, k)
            ready[q][k] = held[q][inverse[to]]
            pltpu.make_async_remote_copy(
                src_ref=ready[q].at[k], dst_ref=outs[q].at[me], send_sem=send.at[2 + q], recv_sem=recv.at[2 + q],
                device_id={"ep": to}, device_id_type=MESH,
            ).start()
            return carry

        lax.fori_loop(1, n, collect, 0)
        ready[q][0] = held[q][inverse[me]]
        pltpu.make_async_copy(ready[q].at[0], outs[q].at[me], local.at[2 + q]).start()

    trade.wait_send()
    for q in range(2):
        pltpu.make_async_copy(ready[q].at[0], outs[q].at[me], local.at[2 + q]).wait()
        pltpu.make_async_remote_copy(
            src_ref=made[q].at[rest], dst_ref=held[q].at[rest], send_sem=send.at[q], recv_sem=recv.at[q],
            device_id={"ep": shifted(me, 1)}, device_id_type=MESH,
        ).wait_send()
        last = pltpu.make_async_remote_copy(
            src_ref=ready[q].at[rest], dst_ref=outs[q].at[rest], send_sem=send.at[2 + q], recv_sem=recv.at[2 + q],
            device_id={"ep": shifted(me, 1)}, device_id_type=MESH,
        )
        last.wait_send()
        last.wait_recv()


def move(n, factor, inverse, kernel_matrix, rows, columns, gate, up):
    half, inner = gate.shape
    pieces = (n, half // n, inner)
    shape = jax.ShapeDtypeStruct(pieces, gate.dtype)
    everywhere, vmem = pl.BlockSpec(memory_space=pl.ANY), pl.BlockSpec(memory_space=pltpu.VMEM)
    return pl.pallas_call(
        functools.partial(move_kernel, n, factor),
        out_shape=(shape, shape),
        in_specs=[pl.BlockSpec(memory_space=pltpu.SMEM), vmem, vmem, vmem, everywhere, everywhere],
        out_specs=(everywhere, everywhere),
        scratch_shapes=[
            pltpu.VMEM((2, half, inner), gate.dtype),
            pltpu.VMEM((2,) + rows.shape, rows.dtype),
        ]
        + [pltpu.VMEM(pieces, gate.dtype)] * 6
        + [
            pltpu.SemaphoreType.DMA((2,)),
            pltpu.SemaphoreType.DMA((4,)),
            pltpu.SemaphoreType.DMA((4,)),
            pltpu.SemaphoreType.DMA((4,)),
            pltpu.SemaphoreType.DMA((2,)),
        ],
        compiler_params=pltpu.CompilerParams(
            collective_id=2, has_side_effects=True, vmem_limit_bytes=48 * 2**20
        ),
        name="move",
    )(inverse, kernel_matrix, rows, columns, gate, up)


def shards(
    dy,
    probs,
    expert_ids,
    copy_choice,
    saved_inputs,
    saved_gate,
    saved_up,
    down_weight,
    gate_weight,
    up_weight,
    new_owner,
):
    first = lax.axis_index("rep") == 0
    experts = lax.axis_size("ep")
    width = dy.shape[1]
    inner = saved_gate.shape[4]
    half = width // 2
    kernel_matrix, rows, columns, inverse = route(
        expert_ids.T, copy_choice.T, probs.T, new_owner.reshape(1, experts), dy, saved_inputs[0, 0],
        saved_gate[0, 0], saved_up[0, 0], down_weight[0],
    )
    factor_rows, columns, inverse = rows.reshape(-1, inner), columns.reshape(-1, half), inverse.reshape(experts)
    own, other = move(
        experts, step_scale * math.sqrt(width), inverse, kernel_matrix, factor_rows, columns, gate_weight[0], up_weight[0]
    )
    new_gate, new_up = jnp.where(first, own, other), jnp.where(first, other, own)
    return new_gate.reshape(1, half, inner), new_up.reshape(1, half, inner)


def solution(mesh):
    in_specs = (
        P("ep", None),
        P("ep", None),
        P("ep", None),
        P("ep", None),
        P("ep", "rep", None, None, None),
        P("ep", "rep", None, None, None),
        P("ep", "rep", None, None, None),
        P("ep", None, "rep"),
        P("ep", "rep", None),
        P("ep", "rep", None),
        P(),
    )
    out_specs = (P("ep", "rep", None), P("ep", "rep", None))
    return jax.shard_map(shards, mesh=mesh, in_specs=in_specs, out_specs=out_specs, check_vma=False)
```

```python
import functools
import math

import jax
import jax.numpy as jnp
from jax import lax
from jax.experimental import pallas as pl
from jax.experimental.pallas import tpu as pltpu
from jax.sharding import PartitionSpec as P

MESH = pl.DeviceIdType.MESH
ITERS = 2

quintic_first = 3.4445
quintic_second = -4.775
quintic_third = 2.0315
step_scale = 2.0
epsilon = 1e-07

GRID = (4, 4, 8)


def shifted(me, k):
    ny, nx, nz = GRID
    y, x, z = me // (nx * nz), (me // nz) % nx, me % nz
    dy, dx, dz = k // (nx * nz), (k // nz) % nx, k % nz
    return (lax.rem(y + dy, ny) * nx + lax.rem(x + dx, nx)) * nz + lax.rem(z + dz, nz)


def dot(a, b, dims):
    return lax.dot_general(a, b, (dims, ((), ())), preferred_element_type=jnp.float32)


CHUNKS = 4


def shift_of(size):
    assert size & (size - 1) == 0
    return size.bit_length() - 1


def selection(table, plane, top, sources, tokens, spots, capacity):
    count = sources * tokens
    lanes = 2 * spots * sources * capacity
    lane = lax.broadcasted_iota(jnp.int32, (1, lanes), 1)
    slot = lane & (capacity - 1)
    source = (lane >> shift_of(capacity)) & (sources - 1)
    spot = (lane >> shift_of(capacity * sources)) & (spots - 1)
    copy = lane >> shift_of(capacity * sources * spots)
    wanted = (((spot * sources + plane) * 2) + copy).astype(jnp.float32)
    blocks, weights = [], []
    for z in range(sources):
        aim = jnp.where(source == z, wanted, -1.0)
        block = jnp.zeros((tokens, lanes), jnp.float32)
        weight = jnp.zeros((tokens, lanes), jnp.float32)
        for k in range(top):
            at = z * 2 * top + k
            hit = table[:, at : at + 1] == aim
            block = jnp.where(hit, 1.0, block)
            weight = jnp.where(hit, table[:, at + top : at + top + 1], weight)
        blocks.append(block)
        weights.append(weight)
    taken = jnp.concatenate(blocks, axis=0)
    weight = jnp.concatenate(weights, axis=0)
    row = lax.broadcasted_iota(jnp.int32, (count, count), 0)
    column = lax.broadcasted_iota(jnp.int32, (count, count), 1)
    before = jnp.where(row > column, 1.0, 0.0).astype(jnp.bfloat16)
    position = dot(before, taken.astype(jnp.bfloat16), ((1,), (0,)))
    mine = (taken > 0.5) & (position == slot.astype(jnp.float32))
    ones = jnp.ones((count, 128), jnp.bfloat16)
    left = jnp.where(mine, weight, 0.0)
    scale = None
    for _ in range(3):
        part = left.astype(jnp.bfloat16)
        left = left - part.astype(jnp.float32)
        term = dot(part, ones, ((0,), (0,)))
        scale = term if scale is None else scale + term
    return jnp.where(mine, 1.0, 0.0).astype(jnp.bfloat16), scale


def remote(src, dst, send, recv, to):
    return pltpu.make_async_remote_copy(
        src_ref=src, dst_ref=dst, send_sem=send, recv_sem=recv, device_id=to, device_id_type=MESH
    )


def route_kernel(
    top, ids_ref, copy_ref, probs_ref, owner_ref, dy_ref, x_ref, g_ref, u_ref, down_ref, k_out, r_out, x_out, inverse_out,
    ids, copies_of, probs, owners, products, slices, spread_of,
    line, meta, gates, keys, sent, routed, raw, inputs, down, rows, other,
    line_send, line_recv, keys_sem, plane_send, plane_recv, near_send, near_recv, pair_send, pair_recv,
    own_sem, piece_sem, small_sem, out_sem,
):
    me = lax.axis_index("ep")
    core = lax.axis_index("rep")
    nz = GRID[2]
    spots = GRID[0] * GRID[1]
    z, spot = me % nz, me // nz
    tokens, width = line.shape[2], line.shape[3]
    capacity = sent.shape[3] // nz
    half = CHUNKS * width
    partner = {"rep": 1 - core}

    def above(k):
        return {"ep": shifted(me, k)}

    count = ids_ref.shape[1]
    small = [
        pltpu.make_async_copy(src, dst, small_sem.at[i])
        for i, (src, dst) in enumerate(
            ((ids_ref, ids), (copy_ref, copies_of), (probs_ref, probs), (owner_ref, owners))
        )
    ]
    for copy in small:
        copy.start()
    barrier = pltpu.get_barrier_semaphore()

    def greet_line(k, carry):
        pl.semaphore_signal(barrier, inc=1, device_id=above(k), device_id_type=MESH)
        return carry

    def greet_plane(k, carry):
        for c in range(2):
            pl.semaphore_signal(
                barrier, inc=1, device_id={"ep": shifted(me, k * nz), "rep": c}, device_id_type=MESH
            )
        return carry

    lax.fori_loop(1, nz, greet_line, 0)
    lax.fori_loop(1, spots, greet_plane, 0)
    pl.semaphore_signal(barrier, inc=1, device_id=partner, device_id_type=MESH)

    def columns(chunk):
        return pl.ds(pl.multiple_of(core * half + chunk * width, width), width)

    own = [pltpu.make_async_copy(dy_ref.at[:, columns(h)], line.at[h, z], own_sem.at[h]) for h in range(CHUNKS)]
    own.append(pltpu.make_async_copy(meta, keys.at[z], own_sem.at[CHUNKS]))
    own.append(pltpu.make_async_copy(x_ref, raw.at[core], own_sem.at[CHUNKS + 1]))
    own.append(pltpu.make_async_copy(down_ref, down.at[core], own_sem.at[CHUNKS + 2]))
    own.append(pltpu.make_async_copy(g_ref, gates.at[0], own_sem.at[CHUNKS + 3]))
    own.append(pltpu.make_async_copy(u_ref, gates.at[1], own_sem.at[CHUNKS + 4]))
    for copy in small[:3]:
        copy.wait()
    keyed = (ids[...] * 2 + copies_of[...]).astype(jnp.float32)
    packed = jnp.concatenate([keyed, probs[...]], axis=0)
    meta[...] = jnp.concatenate([packed, jnp.zeros((2 * top, 128 - count), jnp.float32)], axis=1)
    for copy in own:
        copy.start()
    pl.semaphore_wait(barrier, nz + 2 * (spots - 1))

    def send_keys(k, carry):
        remote(meta, keys.at[z], keys_sem.at[0], keys_sem.at[1], above(k)).start()
        return carry

    for h in range(CHUNKS):

        def send_line(k, carry, h=h):
            remote(dy_ref.at[:, columns(h)], line.at[h, z], line_send.at[h], line_recv.at[h], above(k)).start()
            return carry

        lax.fori_loop(1, nz, send_line, 0)
        if not h:
            lax.fori_loop(1, nz, send_keys, 0)
    swaps = [
        remote(x_ref, raw.at[core], pair_send.at[0], pair_recv.at[0], partner),
        remote(down_ref, down.at[core], pair_send.at[1], pair_recv.at[1], partner),
    ]
    for swap in swaps:
        swap.start()

    others = pl.ds(0, nz - 1)
    all_keys = remote(keys.at[others], keys.at[others], keys_sem.at[0], keys_sem.at[1], above(1))
    all_keys.wait_recv()
    own[CHUNKS].wait()
    table = keys[...].reshape(nz * 2 * top, 128).T
    choose, scale = selection(
        table[:count], z, top, nz, tokens, spots, capacity
    )
    scale = jnp.concatenate([scale] * (width // scale.shape[1]), axis=1)
    for h in range(CHUNKS):
        own[h].wait()
        remote(line.at[h, others], line.at[h, others], line_send.at[h], line_recv.at[h], above(1)).wait_recv()
        picked = dot(choose, line[h].reshape(nz * tokens, width), ((0,), (0,)))
        sent[h] = (picked * scale).astype(jnp.bfloat16).reshape(sent.shape[1:])

        def send_plane(k, carry, h=h):
            to = shifted(me, k * nz)
            for c in range(2):
                remote(
                    sent.at[h, c, to // nz], routed.at[spot, :, columns(h)],
                    plane_send.at[h], plane_recv.at[h], {"ep": to, "rep": c},
                ).start()
            return carry

        lax.fori_loop(1, spots, send_plane, 0)
        remote(
            sent.at[h, 1 - core, spot], routed.at[spot, :, columns(h)], near_send.at[h], near_recv.at[h], partner
        ).start()
        pltpu.make_async_copy(
            sent.at[h, core, spot], routed.at[spot, :, columns(h)], piece_sem.at[h]
        ).start()

    own[CHUNKS + 1].wait()
    swaps[0].wait_recv()
    copies, pairs, features = inputs.shape
    for c in range(2):
        inputs[c] = raw[c].astype(jnp.float32).reshape(pairs, features).astype(jnp.bfloat16)
    everything = inputs[...].reshape(copies * pairs, features)
    products[...] = dot(everything, everything, ((1,), (1,)))
    slices[...] = inputs[:, :, pl.ds(pl.multiple_of(core * half, half), half)]
    own[CHUNKS + 3].wait()
    own[CHUNKS + 4].wait()
    gate_value = gates[0].astype(jnp.float32).reshape(pairs, g_ref.shape[-1])
    up_value = gates[1].astype(jnp.float32).reshape(pairs, u_ref.shape[-1])
    experts = owner_ref.shape[1]
    low = lax.broadcasted_iota(jnp.int32, (experts, experts), 0)
    wide = lax.broadcasted_iota(jnp.int32, (experts, experts), 1).astype(jnp.float32)
    small[3].wait()
    held = jnp.sum(jnp.where(owners[...] == low, wide, 0.0), axis=1, keepdims=True)
    spread_of[...] = jnp.broadcast_to(held, (experts, experts)).T[:1].astype(jnp.int32)
    outgoing = [
        pltpu.make_async_copy(src, dst, out_sem.at[i])
        for i, (src, dst) in enumerate(
            ((products, k_out), (slices, x_out), (spread_of, inverse_out), (rows, r_out))
        )
    ]
    for copy in outgoing[:3]:
        copy.start()
    own[CHUNKS + 2].wait()
    swaps[1].wait_recv()
    near = pl.ds(0, spots - 1)
    hidden = None
    for h in range(CHUNKS):
        pltpu.make_async_copy(sent.at[h, core, spot], routed.at[spot, :, columns(h)], piece_sem.at[h]).wait()
        remote(
            sent.at[h, 1 - core, spot], routed.at[spot, :, columns(h)], near_send.at[h], near_recv.at[h], partner
        ).wait_recv()
        both = sent.at[h, :, near]
        remote(both, both, plane_send.at[h], plane_recv.at[h], partner).wait_recv()
        for c in range(2):
            here = routed[:, :, pl.ds(c * half + h * width, width)].reshape(pairs, width)
            term = dot(here, down[c, :, pl.ds(h * width, width)], ((1,), (1,)))
            hidden = term if hidden is None else hidden + term
    hidden = hidden / math.sqrt(hidden.shape[1])
    sigmoid = jax.nn.sigmoid(gate_value)
    gate_rows = hidden * up_value * sigmoid * (1.0 + gate_value * (1.0 - sigmoid))
    up_rows = hidden * gate_value * sigmoid
    first = core == 0
    rows[core] = jnp.where(first, gate_rows, up_rows).astype(jnp.bfloat16)
    other[...] = jnp.where(first, up_rows, gate_rows).astype(jnp.bfloat16)
    last = remote(other, rows.at[core], pair_send.at[2], pair_recv.at[2], partner)
    last.start()

    last.wait_recv()
    outgoing[3].start()
    all_keys.wait_send()
    for swap in swaps:
        swap.wait_send()
    for h in range(CHUNKS):
        remote(line.at[h, others], line.at[h, others], line_send.at[h], line_recv.at[h], above(1)).wait_send()
        remote(
            sent.at[h, 1 - core, spot], routed.at[spot, :, columns(h)], near_send.at[h], near_recv.at[h], partner
        ).wait_send()
        both = sent.at[h, :, near]
        remote(both, both, plane_send.at[h], plane_recv.at[h], partner).wait_send()
    last.wait_send()
    for copy in outgoing:
        copy.wait()


def route(ids, copies, probs, owner, dy, inputs, gate, up, down):
    top = ids.shape[0]
    pairs, features = inputs.shape[0] * inputs.shape[1], inputs.shape[2]
    inner, half = down.shape
    tokens = dy.shape[0]
    nz, spots = GRID[2], GRID[0] * GRID[1]
    slots = pairs // spots
    width = half // CHUNKS
    everywhere = pl.BlockSpec(memory_space=pl.ANY)
    bf16 = jnp.bfloat16
    semaphores = pltpu.SemaphoreType.DMA
    return pl.pallas_call(
        functools.partial(route_kernel, top),
        out_shape=(
            jax.ShapeDtypeStruct((2 * pairs, 2 * pairs), jnp.float32),
            jax.ShapeDtypeStruct((2, pairs, inner), bf16),
            jax.ShapeDtypeStruct((2, pairs, half), bf16),
            jax.ShapeDtypeStruct(owner.shape, jnp.int32),
        ),
        in_specs=[everywhere] * 9,
        out_specs=(everywhere,) * 4,
        scratch_shapes=[
            pltpu.VMEM(ids.shape, jnp.int32),
            pltpu.VMEM(ids.shape, jnp.int32),
            pltpu.VMEM(ids.shape, jnp.float32),
            pltpu.VMEM(owner.shape, jnp.int32),
            pltpu.VMEM((2 * pairs, 2 * pairs), jnp.float32),
            pltpu.VMEM((2, pairs, half), bf16),
            pltpu.VMEM(owner.shape, jnp.int32),
            pltpu.VMEM((CHUNKS, nz, tokens, width), bf16),
            pltpu.VMEM((2 * top, 128), jnp.float32),
            pltpu.VMEM((2,) + gate.shape, bf16),
            pltpu.VMEM((nz, 2 * top, 128), jnp.float32),
            pltpu.VMEM((CHUNKS, 2, spots, slots, width), bf16),
            pltpu.VMEM((spots, slots, features), bf16),
            pltpu.VMEM((2,) + inputs.shape, bf16),
            pltpu.VMEM((2, pairs, features), bf16),
            pltpu.VMEM((2, inner, half), bf16),
            pltpu.VMEM((2, pairs, inner), bf16),
            pltpu.VMEM((pairs, inner), bf16),
            semaphores((CHUNKS,)),
            semaphores((CHUNKS,)),
            semaphores((2,)),
            semaphores((CHUNKS,)),
            semaphores((CHUNKS,)),
            semaphores((CHUNKS,)),
            semaphores((CHUNKS,)),
            semaphores((3,)),
            semaphores((3,)),
            semaphores((CHUNKS + 5,)),
            semaphores((CHUNKS,)),
            semaphores((4,)),
            semaphores((4,)),
        ],
        compiler_params=pltpu.CompilerParams(
            collective_id=1, has_side_effects=True, vmem_limit_bytes=63 * 2**20
        ),
        name="route",
    )(ids, copies, probs, owner, dy, inputs, gate, up, down)


def orthogonal_factor(kernel_matrix, rows):
    high = kernel_matrix.astype(jnp.bfloat16)
    low = (kernel_matrix - high.astype(jnp.float32)).astype(jnp.bfloat16)
    scale = None
    for repeat in range(ITERS):
        square = dot(rows, rows, ((1,), (1,)))
        if not repeat:
            total = jnp.sqrt(jnp.maximum(jnp.sum(square * kernel_matrix), 0.0))
            scale = 1.0 / (total + epsilon)
            square = square * (scale * scale)
        square = square.astype(jnp.bfloat16)
        gram = dot(square, high, ((1,), (0,))) + dot(square, low, ((1,), (0,)))
        half = gram.astype(jnp.bfloat16)
        poly = quintic_second * gram + quintic_third * dot(half, half, ((1,), (0,)))
        mixed = quintic_first * rows.astype(jnp.float32) + dot(poly.astype(jnp.bfloat16), rows, ((1,), (0,)))
        if not repeat:
            mixed = mixed * scale
        rows = mixed.astype(jnp.bfloat16)
    return rows


def move_kernel(
    n, factor, inverse_ref, k_ref, r_ref, x_ref, gate_ref, up_ref, own_out, other_out,
    inverse, products, begin, columns, weights, factors, made0, made1, held0, held1, ready0, ready1, load, send, recv, local, swap, fetch,
):
    me = lax.axis_index("ep")
    core = lax.axis_index("rep")
    outs, made, held, ready = (own_out, other_out), (made0, made1), (held0, held1), (ready0, ready1)
    ny = GRID[0]
    group = n // ny
    piece = weights.shape[1] // n
    block = group * piece
    rest = pl.ds(0, n - 1)
    partner = {"rep": 1 - core}

    fetches = [
        pltpu.make_async_copy(src, dst, fetch.at[i])
        for i, (src, dst) in enumerate(
            ((k_ref, products), (r_ref, begin), (x_ref, columns), (inverse_ref, inverse))
        )
    ]
    for copy in fetches:
        copy.start()
    barrier = pltpu.get_barrier_semaphore()

    def say(k, carry):
        pl.semaphore_signal(barrier, inc=1, device_id={"ep": shifted(me, k)}, device_id_type=MESH)
        return carry

    lax.fori_loop(1, n, say, 0)
    pl.semaphore_signal(barrier, inc=1, device_id=partner, device_id_type=MESH)

    for c, refs in enumerate(((gate_ref, up_ref), (up_ref, gate_ref))):
        @pl.when(core == c)
        def _(refs=refs):
            for q in range(2):
                pltpu.make_async_copy(refs[q], weights.at[q], load.at[q]).start()

    fetches[0].wait()
    fetches[1].wait()
    factors[0] = orthogonal_factor(products[...], begin[...])
    pl.semaphore_wait(barrier, n)
    trade = pltpu.make_async_remote_copy(
        src_ref=factors.at[0], dst_ref=factors.at[1], send_sem=swap.at[0], recv_sem=swap.at[1],
        device_id=partner, device_id_type=MESH,
    )
    trade.start()
    fetches[2].wait()
    fetches[3].wait()

    for q in range(2):
        pltpu.make_async_copy(gate_ref, weights.at[q], load.at[q]).wait()
        if q:
            trade.wait_recv()

        def spread(k, carry, q=q):
            to = shifted(me, k)
            pltpu.make_async_remote_copy(
                src_ref=made[q].at[to], dst_ref=held[q].at[me], send_sem=send.at[q], recv_sem=recv.at[q],
                device_id={"ep": to}, device_id_type=MESH,
            ).start()
            return carry

        def produce(dy, carry, q=q):
            y = lax.rem(me // group + dy, ny)
            rows = pl.ds(pl.multiple_of(y * block, block), block)
            ortho = dot(columns[:, rows], factors[q], ((0,), (0,)))
            fresh = (weights[q, rows, :].astype(jnp.float32) - factor * ortho).astype(jnp.bfloat16)
            made[q][pl.ds(y * group, group)] = fresh.reshape(group, piece, fresh.shape[1])
            lax.fori_loop(jnp.where(dy == 0, 1, dy * group), (dy + 1) * group, spread, 0)
            return carry

        lax.fori_loop(0, ny, produce, 0)
        pltpu.make_async_copy(made[q].at[me], held[q].at[me], local.at[q]).start()

    for q in range(2):
        pltpu.make_async_copy(made[q].at[me], held[q].at[me], local.at[q]).wait()
        pltpu.make_async_remote_copy(
            src_ref=made[q].at[rest], dst_ref=held[q].at[rest], send_sem=send.at[q], recv_sem=recv.at[q],
            device_id={"ep": shifted(me, 1)}, device_id_type=MESH,
        ).wait_recv()

        def collect(k, carry, q=q):
            to = shifted(me, k)
            ready[q][k] = held[q][inverse[0, to]]
            pltpu.make_async_remote_copy(
                src_ref=ready[q].at[k], dst_ref=outs[q].at[me], send_sem=send.at[2 + q], recv_sem=recv.at[2 + q],
                device_id={"ep": to}, device_id_type=MESH,
            ).start()
            return carry

        lax.fori_loop(1, n, collect, 0)
        ready[q][0] = held[q][inverse[0, me]]
        pltpu.make_async_copy(ready[q].at[0], outs[q].at[me], local.at[2 + q]).start()

    trade.wait_send()
    for q in range(2):
        pltpu.make_async_copy(ready[q].at[0], outs[q].at[me], local.at[2 + q]).wait()
        pltpu.make_async_remote_copy(
            src_ref=made[q].at[rest], dst_ref=held[q].at[rest], send_sem=send.at[q], recv_sem=recv.at[q],
            device_id={"ep": shifted(me, 1)}, device_id_type=MESH,
        ).wait_send()
        last = pltpu.make_async_remote_copy(
            src_ref=ready[q].at[rest], dst_ref=outs[q].at[rest], send_sem=send.at[2 + q], recv_sem=recv.at[2 + q],
            device_id={"ep": shifted(me, 1)}, device_id_type=MESH,
        )
        last.wait_send()
        last.wait_recv()


def move(n, factor, inverse, kernel_matrix, rows, columns, gate, up):
    half, inner = gate.shape
    pieces = (n, half // n, inner)
    shape = jax.ShapeDtypeStruct(pieces, gate.dtype)
    everywhere = pl.BlockSpec(memory_space=pl.ANY)
    return pl.pallas_call(
        functools.partial(move_kernel, n, factor),
        out_shape=(shape, shape),
        in_specs=[everywhere] * 6,
        out_specs=(everywhere, everywhere),
        scratch_shapes=[
            pltpu.SMEM(inverse.shape, jnp.int32),
            pltpu.VMEM(kernel_matrix.shape, jnp.float32),
            pltpu.VMEM(rows.shape, rows.dtype),
            pltpu.VMEM(columns.shape, columns.dtype),
            pltpu.VMEM((2, half, inner), gate.dtype),
            pltpu.VMEM((2,) + rows.shape, rows.dtype),
        ]
        + [pltpu.VMEM(pieces, gate.dtype)] * 6
        + [
            pltpu.SemaphoreType.DMA((2,)),
            pltpu.SemaphoreType.DMA((4,)),
            pltpu.SemaphoreType.DMA((4,)),
            pltpu.SemaphoreType.DMA((4,)),
            pltpu.SemaphoreType.DMA((2,)),
            pltpu.SemaphoreType.DMA((4,)),
        ],
        compiler_params=pltpu.CompilerParams(
            collective_id=2, has_side_effects=True, vmem_limit_bytes=63 * 2**20
        ),
        name="move",
    )(inverse, kernel_matrix, rows, columns, gate, up)


def shards(
    dy,
    probs,
    expert_ids,
    copy_choice,
    saved_inputs,
    saved_gate,
    saved_up,
    down_weight,
    gate_weight,
    up_weight,
    new_owner,
):
    first = lax.axis_index("rep") == 0
    experts = lax.axis_size("ep")
    width = dy.shape[1]
    inner = saved_gate.shape[4]
    half = width // 2
    kernel_matrix, rows, columns, inverse = route(
        expert_ids.T, copy_choice.T, probs.T, new_owner.reshape(1, experts), dy, saved_inputs[0, 0],
        saved_gate[0, 0], saved_up[0, 0], down_weight[0],
    )
    factor_rows, columns = rows.reshape(-1, inner), columns.reshape(-1, half)
    own, other = move(
        experts, step_scale * math.sqrt(width), inverse, kernel_matrix, factor_rows, columns, gate_weight[0], up_weight[0]
    )
    new_gate, new_up = jnp.where(first, own, other), jnp.where(first, other, own)
    return new_gate.reshape(1, half, inner), new_up.reshape(1, half, inner)


def solution(mesh):
    in_specs = (
        P("ep", None),
        P("ep", None),
        P("ep", None),
        P("ep", None),
        P("ep", "rep", None, None, None),
        P("ep", "rep", None, None, None),
        P("ep", "rep", None, None, None),
        P("ep", None, "rep"),
        P("ep", "rep", None),
        P("ep", "rep", None),
        P(),
    )
    out_specs = (P("ep", "rep", None), P("ep", "rep", None))
    return jax.shard_map(shards, mesh=mesh, in_specs=in_specs, out_specs=out_specs, check_vma=False)
```

```python
import functools
import math

import jax
import jax.numpy as jnp
from jax import lax
from jax.experimental import pallas as pl
from jax.experimental.pallas import tpu as pltpu
from jax.sharding import PartitionSpec as P

MESH = pl.DeviceIdType.MESH
ITERS = 2

quintic_first = 3.4445
quintic_second = -4.775
quintic_third = 2.0315
step_scale = 2.0
epsilon = 1e-07

GRID = (4, 4, 8)


def shifted(me, k):
    ny, nx, nz = GRID
    y, x, z = me // (nx * nz), (me // nz) % nx, me % nz
    dy, dx, dz = k // (nx * nz), (k // nz) % nx, k % nz
    return (lax.rem(y + dy, ny) * nx + lax.rem(x + dx, nx)) * nz + lax.rem(z + dz, nz)


def dot(a, b, dims):
    return lax.dot_general(a, b, (dims, ((), ())), preferred_element_type=jnp.float32)


CHUNKS = 4


def shift_of(size):
    assert size & (size - 1) == 0
    return size.bit_length() - 1


def selection(table, plane, top, sources, tokens, spots, capacity):
    count = sources * tokens
    lanes = 2 * spots * sources * capacity
    lane = lax.broadcasted_iota(jnp.int32, (1, lanes), 1)
    slot = lane & (capacity - 1)
    source = (lane >> shift_of(capacity)) & (sources - 1)
    spot = (lane >> shift_of(capacity * sources)) & (spots - 1)
    copy = lane >> shift_of(capacity * sources * spots)
    wanted = (((spot * sources + plane) * 2) + copy).astype(jnp.float32)
    blocks, weights = [], []
    for z in range(sources):
        aim = jnp.where(source == z, wanted, -1.0)
        block = jnp.zeros((tokens, lanes), jnp.float32)
        weight = jnp.zeros((tokens, lanes), jnp.float32)
        for k in range(top):
            at = z * 2 * top + k
            hit = table[:, at : at + 1] == aim
            block = jnp.where(hit, 1.0, block)
            weight = jnp.where(hit, table[:, at + top : at + top + 1], weight)
        blocks.append(block)
        weights.append(weight)
    taken = jnp.concatenate(blocks, axis=0)
    weight = jnp.concatenate(weights, axis=0)
    row = lax.broadcasted_iota(jnp.int32, (count, count), 0)
    column = lax.broadcasted_iota(jnp.int32, (count, count), 1)
    before = jnp.where(row > column, 1.0, 0.0).astype(jnp.bfloat16)
    position = dot(before, taken.astype(jnp.bfloat16), ((1,), (0,)))
    mine = (taken > 0.5) & (position == slot.astype(jnp.float32))
    ones = jnp.ones((count, 128), jnp.bfloat16)
    left = jnp.where(mine, weight, 0.0)
    scale = None
    for _ in range(3):
        part = left.astype(jnp.bfloat16)
        left = left - part.astype(jnp.float32)
        term = dot(part, ones, ((0,), (0,)))
        scale = term if scale is None else scale + term
    return jnp.where(mine, 1.0, 0.0).astype(jnp.bfloat16), scale


def remote(src, dst, send, recv, to):
    return pltpu.make_async_remote_copy(
        src_ref=src, dst_ref=dst, send_sem=send, recv_sem=recv, device_id=to, device_id_type=MESH
    )


def orthogonal_factor(kernel_matrix, rows):
    high = kernel_matrix.astype(jnp.bfloat16)
    low = (kernel_matrix - high.astype(jnp.float32)).astype(jnp.bfloat16)
    scale = None
    for repeat in range(ITERS):
        square = dot(rows, rows, ((1,), (1,)))
        if not repeat:
            total = jnp.sqrt(jnp.maximum(jnp.sum(square * kernel_matrix), 0.0))
            scale = 1.0 / (total + epsilon)
            square = square * (scale * scale)
        square = square.astype(jnp.bfloat16)
        gram = dot(square, high, ((1,), (0,))) + dot(square, low, ((1,), (0,)))
        half = gram.astype(jnp.bfloat16)
        poly = quintic_second * gram + quintic_third * dot(half, half, ((1,), (0,)))
        mixed = quintic_first * rows.astype(jnp.float32) + dot(poly.astype(jnp.bfloat16), rows, ((1,), (0,)))
        if not repeat:
            mixed = mixed * scale
        rows = mixed.astype(jnp.bfloat16)
    return rows


def step_kernel(
    top, factor, ids_ref, copy_ref, probs_ref, inverse_ref, dy_ref, x_ref, g_ref, u_ref, down_ref, gate_ref, up_ref,
    own_out, other_out,
    ids, copies_of, probs, products, slices,
    line, meta, gates, keys, sent, routed, raw, inputs, down, rows, other,
    line_send, line_recv, keys_sem, plane_send, plane_recv, near_send, near_recv, pair_send, pair_recv,
    own_sem, piece_sem, small_sem,
    inverse, weights, factors, made0, made1, held0, held1, ready0, ready1,
    load, send, recv, local, swap_sem, index_sem,
):
    me = lax.axis_index("ep")
    core = lax.axis_index("rep")
    nz = GRID[2]
    spots = GRID[0] * GRID[1]
    z, spot = me % nz, me // nz
    tokens, width = line.shape[2], line.shape[3]
    capacity = sent.shape[3] // nz
    half = CHUNKS * width
    partner = {"rep": 1 - core}

    def above(k):
        return {"ep": shifted(me, k)}

    count = ids_ref.shape[1]
    small = [
        pltpu.make_async_copy(src, dst, small_sem.at[i])
        for i, (src, dst) in enumerate(
            ((ids_ref, ids), (copy_ref, copies_of), (probs_ref, probs))
        )
    ]
    for copy in small:
        copy.start()
    indices = pltpu.make_async_copy(inverse_ref, inverse, index_sem)
    indices.start()
    barrier = pltpu.get_barrier_semaphore()

    def greet_line(k, carry):
        pl.semaphore_signal(barrier, inc=1, device_id=above(k), device_id_type=MESH)
        return carry

    def greet_plane(k, carry):
        for c in range(2):
            pl.semaphore_signal(
                barrier, inc=1, device_id={"ep": shifted(me, k * nz), "rep": c}, device_id_type=MESH
            )
        return carry

    lax.fori_loop(1, nz, greet_line, 0)
    lax.fori_loop(1, spots, greet_plane, 0)
    pl.semaphore_signal(barrier, inc=1, device_id=partner, device_id_type=MESH)

    def columns(chunk):
        return pl.ds(pl.multiple_of(core * half + chunk * width, width), width)

    own = [pltpu.make_async_copy(dy_ref.at[:, columns(h)], line.at[h, z], own_sem.at[h]) for h in range(CHUNKS)]
    own.append(pltpu.make_async_copy(meta, keys.at[z], own_sem.at[CHUNKS]))
    own.append(pltpu.make_async_copy(x_ref, raw.at[core], own_sem.at[CHUNKS + 1]))
    own.append(pltpu.make_async_copy(down_ref, down.at[core], own_sem.at[CHUNKS + 2]))
    own.append(pltpu.make_async_copy(g_ref, gates.at[0], own_sem.at[CHUNKS + 3]))
    own.append(pltpu.make_async_copy(u_ref, gates.at[1], own_sem.at[CHUNKS + 4]))
    for copy in small:
        copy.wait()
    keyed = (ids[...] * 2 + copies_of[...]).astype(jnp.float32)
    packed = jnp.concatenate([keyed, probs[...]], axis=0)
    meta[...] = jnp.concatenate([packed, jnp.zeros((2 * top, 128 - count), jnp.float32)], axis=1)
    for copy in own:
        copy.start()
    for c, refs in enumerate(((gate_ref, up_ref), (up_ref, gate_ref))):
        @pl.when(core == c)
        def _(refs=refs):
            for q in range(2):
                pltpu.make_async_copy(refs[q], weights.at[q], load.at[q]).start()

    pl.semaphore_wait(barrier, nz + 2 * (spots - 1))

    def send_keys(k, carry):
        remote(meta, keys.at[z], keys_sem.at[0], keys_sem.at[1], above(k)).start()
        return carry

    for h in range(CHUNKS):

        def send_line(k, carry, h=h):
            remote(dy_ref.at[:, columns(h)], line.at[h, z], line_send.at[h], line_recv.at[h], above(k)).start()
            return carry

        lax.fori_loop(1, nz, send_line, 0)
        if not h:
            lax.fori_loop(1, nz, send_keys, 0)
    swaps = [
        remote(x_ref, raw.at[core], pair_send.at[0], pair_recv.at[0], partner),
        remote(down_ref, down.at[core], pair_send.at[1], pair_recv.at[1], partner),
    ]
    for swap in swaps:
        swap.start()

    others = pl.ds(0, nz - 1)
    all_keys = remote(keys.at[others], keys.at[others], keys_sem.at[0], keys_sem.at[1], above(1))
    all_keys.wait_recv()
    own[CHUNKS].wait()
    table = keys[...].reshape(nz * 2 * top, 128).T
    choose, scale = selection(
        table[:count], z, top, nz, tokens, spots, capacity
    )
    scale = jnp.concatenate([scale] * (width // scale.shape[1]), axis=1)
    for h in range(CHUNKS):
        own[h].wait()
        remote(line.at[h, others], line.at[h, others], line_send.at[h], line_recv.at[h], above(1)).wait_recv()
        picked = dot(choose, line[h].reshape(nz * tokens, width), ((0,), (0,)))
        sent[h] = (picked * scale).astype(jnp.bfloat16).reshape(sent.shape[1:])

        def send_plane(k, carry, h=h):
            to = shifted(me, k * nz)
            for c in range(2):
                remote(
                    sent.at[h, c, to // nz], routed.at[spot, :, columns(h)],
                    plane_send.at[h], plane_recv.at[h], {"ep": to, "rep": c},
                ).start()
            return carry

        lax.fori_loop(1, spots, send_plane, 0)
        remote(
            sent.at[h, 1 - core, spot], routed.at[spot, :, columns(h)], near_send.at[h], near_recv.at[h], partner
        ).start()
        pltpu.make_async_copy(
            sent.at[h, core, spot], routed.at[spot, :, columns(h)], piece_sem.at[h]
        ).start()

    own[CHUNKS + 1].wait()
    swaps[0].wait_recv()
    copies, pairs, features = inputs.shape
    for c in range(2):
        inputs[c] = raw[c].astype(jnp.float32).reshape(pairs, features).astype(jnp.bfloat16)
    everything = inputs[...].reshape(copies * pairs, features)
    products[...] = dot(everything, everything, ((1,), (1,)))
    slices[...] = inputs[:, :, pl.ds(pl.multiple_of(core * half, half), half)]
    own[CHUNKS + 3].wait()
    own[CHUNKS + 4].wait()
    gate_value = gates[0].astype(jnp.float32).reshape(pairs, g_ref.shape[-1])
    up_value = gates[1].astype(jnp.float32).reshape(pairs, u_ref.shape[-1])
    own[CHUNKS + 2].wait()
    swaps[1].wait_recv()
    near = pl.ds(0, spots - 1)
    hidden = None
    for h in range(CHUNKS):
        pltpu.make_async_copy(sent.at[h, core, spot], routed.at[spot, :, columns(h)], piece_sem.at[h]).wait()
        remote(
            sent.at[h, 1 - core, spot], routed.at[spot, :, columns(h)], near_send.at[h], near_recv.at[h], partner
        ).wait_recv()
        both = sent.at[h, :, near]
        remote(both, both, plane_send.at[h], plane_recv.at[h], partner).wait_recv()
        for c in range(2):
            here = routed[:, :, pl.ds(c * half + h * width, width)].reshape(pairs, width)
            term = dot(here, down[c, :, pl.ds(h * width, width)], ((1,), (1,)))
            hidden = term if hidden is None else hidden + term
    hidden = hidden / math.sqrt(hidden.shape[1])
    sigmoid = jax.nn.sigmoid(gate_value)
    gate_rows = hidden * up_value * sigmoid * (1.0 + gate_value * (1.0 - sigmoid))
    up_rows = hidden * gate_value * sigmoid
    first = core == 0
    rows[core] = jnp.where(first, gate_rows, up_rows).astype(jnp.bfloat16)
    other[...] = jnp.where(first, up_rows, gate_rows).astype(jnp.bfloat16)
    swapped = remote(other, rows.at[core], pair_send.at[2], pair_recv.at[2], partner)
    swapped.start()

    swapped.wait_recv()

    n = made0.shape[0]
    outs, made, held, ready = (own_out, other_out), (made0, made1), (held0, held1), (ready0, ready1)
    ny = GRID[0]
    group = n // ny
    piece = weights.shape[1] // n
    block = group * piece
    rest = pl.ds(0, n - 1)

    factors[0] = orthogonal_factor(products[...], rows[...].reshape(2 * pairs, rows.shape[2]))
    trade = pltpu.make_async_remote_copy(
        src_ref=factors.at[0], dst_ref=factors.at[1], send_sem=swap_sem.at[0], recv_sem=swap_sem.at[1],
        device_id=partner, device_id_type=MESH,
    )
    trade.start()
    indices.wait()

    for q in range(2):
        pltpu.make_async_copy(gate_ref, weights.at[q], load.at[q]).wait()
        if q:
            trade.wait_recv()

        def spread(k, carry, q=q):
            to = shifted(me, k)
            pltpu.make_async_remote_copy(
                src_ref=made[q].at[to], dst_ref=held[q].at[me], send_sem=send.at[q], recv_sem=recv.at[q],
                device_id={"ep": to}, device_id_type=MESH,
            ).start()
            return carry

        def produce(dy, carry, q=q):
            y = lax.rem(me // group + dy, ny)
            span = pl.ds(pl.multiple_of(y * block, block), block)
            ortho = dot(slices[:, :, span].reshape(2 * pairs, block), factors[q], ((0,), (0,)))
            fresh = (weights[q, span, :].astype(jnp.float32) - factor * ortho).astype(jnp.bfloat16)
            made[q][pl.ds(y * group, group)] = fresh.reshape(group, piece, fresh.shape[1])
            lax.fori_loop(jnp.where(dy == 0, 1, dy * group), (dy + 1) * group, spread, 0)
            return carry

        lax.fori_loop(0, ny, produce, 0)
        pltpu.make_async_copy(made[q].at[me], held[q].at[me], local.at[q]).start()

    for q in range(2):
        pltpu.make_async_copy(made[q].at[me], held[q].at[me], local.at[q]).wait()
        pltpu.make_async_remote_copy(
            src_ref=made[q].at[rest], dst_ref=held[q].at[rest], send_sem=send.at[q], recv_sem=recv.at[q],
            device_id={"ep": shifted(me, 1)}, device_id_type=MESH,
        ).wait_recv()

        def collect(k, carry, q=q):
            to = shifted(me, k)
            ready[q][k] = held[q][inverse[0, to]]
            pltpu.make_async_remote_copy(
                src_ref=ready[q].at[k], dst_ref=outs[q].at[me], send_sem=send.at[2 + q], recv_sem=recv.at[2 + q],
                device_id={"ep": to}, device_id_type=MESH,
            ).start()
            return carry

        lax.fori_loop(1, n, collect, 0)
        ready[q][0] = held[q][inverse[0, me]]
        pltpu.make_async_copy(ready[q].at[0], outs[q].at[me], local.at[2 + q]).start()

    trade.wait_send()
    for q in range(2):
        pltpu.make_async_copy(ready[q].at[0], outs[q].at[me], local.at[2 + q]).wait()
        pltpu.make_async_remote_copy(
            src_ref=made[q].at[rest], dst_ref=held[q].at[rest], send_sem=send.at[q], recv_sem=recv.at[q],
            device_id={"ep": shifted(me, 1)}, device_id_type=MESH,
        ).wait_send()
        last = pltpu.make_async_remote_copy(
            src_ref=ready[q].at[rest], dst_ref=outs[q].at[rest], send_sem=send.at[2 + q], recv_sem=recv.at[2 + q],
            device_id={"ep": shifted(me, 1)}, device_id_type=MESH,
        )
        last.wait_send()
        last.wait_recv()

    all_keys.wait_send()
    for swap in swaps:
        swap.wait_send()
    for h in range(CHUNKS):
        remote(line.at[h, others], line.at[h, others], line_send.at[h], line_recv.at[h], above(1)).wait_send()
        remote(
            sent.at[h, 1 - core, spot], routed.at[spot, :, columns(h)], near_send.at[h], near_recv.at[h], partner
        ).wait_send()
        both = sent.at[h, :, near]
        remote(both, both, plane_send.at[h], plane_recv.at[h], partner).wait_send()
    swapped.wait_send()


def step(factor, ids, copies, probs, inverse, dy, inputs, gate, up, down, gate_matrix, up_matrix):
    top = ids.shape[0]
    pairs, features = inputs.shape[0] * inputs.shape[1], inputs.shape[2]
    inner, half = down.shape
    tokens = dy.shape[0]
    nz, spots = GRID[2], GRID[0] * GRID[1]
    slots = pairs // spots
    width = half // CHUNKS
    everywhere = pl.BlockSpec(memory_space=pl.ANY)
    bf16 = jnp.bfloat16
    experts = inverse.shape[1]
    shape = jax.ShapeDtypeStruct((experts, half // experts, inner), bf16)
    semaphores = pltpu.SemaphoreType.DMA
    return pl.pallas_call(
        functools.partial(step_kernel, top, factor),
        out_shape=(shape, shape),
        in_specs=[everywhere] * 11,
        out_specs=(everywhere, everywhere),
        scratch_shapes=[
            pltpu.VMEM(ids.shape, jnp.int32),
            pltpu.VMEM(ids.shape, jnp.int32),
            pltpu.VMEM(ids.shape, jnp.float32),
            pltpu.VMEM((2 * pairs, 2 * pairs), jnp.float32),
            pltpu.VMEM((2, pairs, half), bf16),
            pltpu.VMEM((CHUNKS, nz, tokens, width), bf16),
            pltpu.VMEM((2 * top, 128), jnp.float32),
            pltpu.VMEM((2,) + gate.shape, bf16),
            pltpu.VMEM((nz, 2 * top, 128), jnp.float32),
            pltpu.VMEM((CHUNKS, 2, spots, slots, width), bf16),
            pltpu.VMEM((spots, slots, features), bf16),
            pltpu.VMEM((2,) + inputs.shape, bf16),
            pltpu.VMEM((2, pairs, features), bf16),
            pltpu.VMEM((2, inner, half), bf16),
            pltpu.VMEM((2, pairs, inner), bf16),
            pltpu.VMEM((pairs, inner), bf16),
            semaphores((CHUNKS,)),
            semaphores((CHUNKS,)),
            semaphores((2,)),
            semaphores((CHUNKS,)),
            semaphores((CHUNKS,)),
            semaphores((CHUNKS,)),
            semaphores((CHUNKS,)),
            semaphores((3,)),
            semaphores((3,)),
            semaphores((CHUNKS + 5,)),
            semaphores((CHUNKS,)),
            semaphores((3,)),
            pltpu.SMEM(inverse.shape, jnp.int32),
            pltpu.VMEM((2, half, inner), bf16),
            pltpu.VMEM((2, 2 * pairs, inner), bf16),
        ]
        + [pltpu.VMEM(shape.shape, bf16)] * 6
        + [
            semaphores((2,)),
            semaphores((4,)),
            semaphores((4,)),
            semaphores((4,)),
            semaphores((2,)),
            semaphores,
        ],
        compiler_params=pltpu.CompilerParams(
            collective_id=1, has_side_effects=True, vmem_limit_bytes=60 * 2**20
        ),
        name="step",
    )(ids, copies, probs, inverse, dy, inputs, gate, up, down, gate_matrix, up_matrix)


def shards(
    dy,
    probs,
    expert_ids,
    copy_choice,
    saved_inputs,
    saved_gate,
    saved_up,
    down_weight,
    gate_weight,
    up_weight,
    new_owner,
):
    first = lax.axis_index("rep") == 0
    experts = lax.axis_size("ep")
    width = dy.shape[1]
    inner = saved_gate.shape[4]
    half = width // 2
    expert = jnp.arange(experts, dtype=jnp.int32)
    inverse = jnp.sum(
        jnp.where(new_owner[:, None] == expert[None, :], expert[:, None], 0), axis=0, dtype=jnp.int32
    ).reshape(1, experts)
    own, other = step(
        step_scale * math.sqrt(width), expert_ids.T, copy_choice.T, probs.T, inverse, dy,
        saved_inputs[0, 0], saved_gate[0, 0], saved_up[0, 0], down_weight[0], gate_weight[0], up_weight[0],
    )
    new_gate, new_up = jnp.where(first, own, other), jnp.where(first, other, own)
    return new_gate.reshape(1, half, inner), new_up.reshape(1, half, inner)


def solution(mesh):
    in_specs = (
        P("ep", None),
        P("ep", None),
        P("ep", None),
        P("ep", None),
        P("ep", "rep", None, None, None),
        P("ep", "rep", None, None, None),
        P("ep", "rep", None, None, None),
        P("ep", None, "rep"),
        P("ep", "rep", None),
        P("ep", "rep", None),
        P(),
    )
    out_specs = (P("ep", "rep", None), P("ep", "rep", None))
    return jax.shard_map(shards, mesh=mesh, in_specs=in_specs, out_specs=out_specs, check_vma=False)
```

```python
import functools
import math

import jax
import jax.numpy as jnp
from jax import lax
from jax.experimental import pallas as pl
from jax.experimental.pallas import tpu as pltpu
from jax.sharding import PartitionSpec as P

MESH = pl.DeviceIdType.MESH
ITERS = 2

quintic_first = 3.4445
quintic_second = -4.775
quintic_third = 2.0315
step_scale = 2.0
epsilon = 1e-07

GRID = (4, 4, 8)


def shifted(me, k):
    ny, nx, nz = GRID
    y, x, z = me // (nx * nz), (me // nz) % nx, me % nz
    dy, dx, dz = k // (nx * nz), (k // nz) % nx, k % nz
    return (lax.rem(y + dy, ny) * nx + lax.rem(x + dx, nx)) * nz + lax.rem(z + dz, nz)


def dot(a, b, dims):
    return lax.dot_general(a, b, (dims, ((), ())), preferred_element_type=jnp.float32)


CHUNKS = 4


def shift_of(size):
    assert size & (size - 1) == 0
    return size.bit_length() - 1


def selection(table, plane, top, sources, tokens, spots, capacity):
    count = sources * tokens
    lanes = 2 * spots * sources * capacity
    lane = lax.broadcasted_iota(jnp.int32, (1, lanes), 1)
    slot = lane & (capacity - 1)
    source = (lane >> shift_of(capacity)) & (sources - 1)
    spot = (lane >> shift_of(capacity * sources)) & (spots - 1)
    copy = lane >> shift_of(capacity * sources * spots)
    wanted = (((spot * sources + plane) * 2) + copy).astype(jnp.float32)
    blocks, weights = [], []
    for z in range(sources):
        aim = jnp.where(source == z, wanted, -1.0)
        block = jnp.zeros((tokens, lanes), jnp.float32)
        weight = jnp.zeros((tokens, lanes), jnp.float32)
        for k in range(top):
            at = z * 2 * top + k
            hit = table[:, at : at + 1] == aim
            block = jnp.where(hit, 1.0, block)
            weight = jnp.where(hit, table[:, at + top : at + top + 1], weight)
        blocks.append(block)
        weights.append(weight)
    taken = jnp.concatenate(blocks, axis=0)
    weight = jnp.concatenate(weights, axis=0)
    row = lax.broadcasted_iota(jnp.int32, (count, count), 0)
    column = lax.broadcasted_iota(jnp.int32, (count, count), 1)
    before = jnp.where(row > column, 1.0, 0.0).astype(jnp.bfloat16)
    position = dot(before, taken.astype(jnp.bfloat16), ((1,), (0,)))
    mine = (taken > 0.5) & (position == slot.astype(jnp.float32))
    ones = jnp.ones((count, 128), jnp.bfloat16)
    left = jnp.where(mine, weight, 0.0)
    scale = None
    for _ in range(3):
        part = left.astype(jnp.bfloat16)
        left = left - part.astype(jnp.float32)
        term = dot(part, ones, ((0,), (0,)))
        scale = term if scale is None else scale + term
    return jnp.where(mine, 1.0, 0.0).astype(jnp.bfloat16), scale


def remote(src, dst, send, recv, to):
    return pltpu.make_async_remote_copy(
        src_ref=src, dst_ref=dst, send_sem=send, recv_sem=recv, device_id=to, device_id_type=MESH
    )


def orthogonal_factor(kernel_matrix, rows):
    high = kernel_matrix.astype(jnp.bfloat16)
    low = (kernel_matrix - high.astype(jnp.float32)).astype(jnp.bfloat16)
    scale = None
    for repeat in range(ITERS):
        square = dot(rows, rows, ((1,), (1,)))
        if not repeat:
            total = jnp.sqrt(jnp.maximum(jnp.sum(square * kernel_matrix), 0.0))
            scale = 1.0 / (total + epsilon)
            square = square * (scale * scale)
        square = square.astype(jnp.bfloat16)
        gram = dot(square, high, ((1,), (0,))) + dot(square, low, ((1,), (0,)))
        half = gram.astype(jnp.bfloat16)
        poly = quintic_second * gram + quintic_third * dot(half, half, ((1,), (0,)))
        mixed = quintic_first * rows.astype(jnp.float32) + dot(poly.astype(jnp.bfloat16), rows, ((1,), (0,)))
        if not repeat:
            mixed = mixed * scale
        rows = mixed.astype(jnp.bfloat16)
    return rows


def step_kernel(
    top, factor, ids_ref, copy_ref, probs_ref, inverse_ref, dy_ref, x_ref, g_ref, u_ref, down_ref, gate_ref, up_ref,
    own_out, other_out,
    ids, copies_of, probs, products, slices,
    line, meta, gates, keys, sent, routed, raw, inputs, down, rows, other,
    line_send, line_recv, keys_sem, plane_send, plane_recv, near_send, near_recv, pair_send, pair_recv,
    own_sem, piece_sem, small_sem,
    inverse, weights, factors, made0, made1, held0, held1, ready0, ready1,
    load, send, recv, local, swap_sem, index_sem,
):
    me = lax.axis_index("ep")
    core = lax.axis_index("rep")
    nz = GRID[2]
    spots = GRID[0] * GRID[1]
    z, spot = me % nz, me // nz
    tokens, width = line.shape[2], line.shape[3]
    capacity = sent.shape[3] // nz
    half = CHUNKS * width
    partner = {"rep": 1 - core}

    def above(k):
        return {"ep": shifted(me, k)}

    count = ids_ref.shape[1]
    small = [
        pltpu.make_async_copy(src, dst, small_sem.at[i])
        for i, (src, dst) in enumerate(
            ((ids_ref, ids), (copy_ref, copies_of), (probs_ref, probs))
        )
    ]
    for copy in small:
        copy.start()
    indices = pltpu.make_async_copy(inverse_ref, inverse, index_sem)
    indices.start()
    barrier = pltpu.get_barrier_semaphore()

    def greet_line(k, carry):
        pl.semaphore_signal(barrier, inc=1, device_id=above(k), device_id_type=MESH)
        return carry

    def greet_plane(k, carry):
        for c in range(2):
            pl.semaphore_signal(
                barrier, inc=1, device_id={"ep": shifted(me, k * nz), "rep": c}, device_id_type=MESH
            )
        return carry

    lax.fori_loop(1, nz, greet_line, 0)
    lax.fori_loop(1, spots, greet_plane, 0)
    pl.semaphore_signal(barrier, inc=1, device_id=partner, device_id_type=MESH)

    def columns(chunk):
        return pl.ds(pl.multiple_of(core * half + chunk * width, width), width)

    own = [pltpu.make_async_copy(dy_ref.at[:, columns(h)], line.at[h, z], own_sem.at[h]) for h in range(CHUNKS)]
    own.append(pltpu.make_async_copy(meta, keys.at[z], own_sem.at[CHUNKS]))
    own.append(pltpu.make_async_copy(x_ref, raw.at[core], own_sem.at[CHUNKS + 1]))
    own.append(pltpu.make_async_copy(down_ref, down.at[core], own_sem.at[CHUNKS + 2]))
    own.append(pltpu.make_async_copy(g_ref, gates.at[0], own_sem.at[CHUNKS + 3]))
    own.append(pltpu.make_async_copy(u_ref, gates.at[1], own_sem.at[CHUNKS + 4]))
    for copy in small:
        copy.wait()
    keyed = (ids[...] * 2 + copies_of[...]).astype(jnp.float32)
    packed = jnp.concatenate([keyed, probs[...]], axis=0)
    meta[...] = jnp.concatenate([packed, jnp.zeros((2 * top, 128 - count), jnp.float32)], axis=1)
    for copy in own:
        copy.start()
    pl.semaphore_wait(barrier, nz + 2 * (spots - 1))

    def send_keys(k, carry):
        remote(meta, keys.at[z], keys_sem.at[0], keys_sem.at[1], above(k)).start()
        return carry

    for h in range(CHUNKS):

        def send_line(k, carry, h=h):
            remote(dy_ref.at[:, columns(h)], line.at[h, z], line_send.at[h], line_recv.at[h], above(k)).start()
            return carry

        lax.fori_loop(1, nz, send_line, 0)
        if not h:
            lax.fori_loop(1, nz, send_keys, 0)
    swaps = [
        remote(x_ref, raw.at[core], pair_send.at[0], pair_recv.at[0], partner),
        remote(down_ref, down.at[core], pair_send.at[1], pair_recv.at[1], partner),
    ]
    for swap in swaps:
        swap.start()

    for c, refs in enumerate(((gate_ref, up_ref), (up_ref, gate_ref))):
        @pl.when(core == c)
        def _(refs=refs):
            for q in range(2):
                pltpu.make_async_copy(refs[q], weights.at[q], load.at[q]).start()


    others = pl.ds(0, nz - 1)
    all_keys = remote(keys.at[others], keys.at[others], keys_sem.at[0], keys_sem.at[1], above(1))
    all_keys.wait_recv()
    own[CHUNKS].wait()
    table = keys[...].reshape(nz * 2 * top, 128).T
    choose, scale = selection(
        table[:count], z, top, nz, tokens, spots, capacity
    )
    scale = jnp.concatenate([scale] * (width // scale.shape[1]), axis=1)
    for h in range(CHUNKS):
        own[h].wait()
        remote(line.at[h, others], line.at[h, others], line_send.at[h], line_recv.at[h], above(1)).wait_recv()
        picked = dot(choose, line[h].reshape(nz * tokens, width), ((0,), (0,)))
        sent[h] = (picked * scale).astype(jnp.bfloat16).reshape(sent.shape[1:])

        def send_plane(k, carry, h=h):
            to = shifted(me, k * nz)
            for c in range(2):
                remote(
                    sent.at[h, c, to // nz], routed.at[spot, :, columns(h)],
                    plane_send.at[h], plane_recv.at[h], {"ep": to, "rep": c},
                ).start()
            return carry

        lax.fori_loop(1, spots, send_plane, 0)
        remote(
            sent.at[h, 1 - core, spot], routed.at[spot, :, columns(h)], near_send.at[h], near_recv.at[h], partner
        ).start()
        pltpu.make_async_copy(
            sent.at[h, core, spot], routed.at[spot, :, columns(h)], piece_sem.at[h]
        ).start()

    own[CHUNKS + 1].wait()
    swaps[0].wait_recv()
    copies, pairs, features = inputs.shape
    for c in range(2):
        inputs[c] = raw[c].astype(jnp.float32).reshape(pairs, features).astype(jnp.bfloat16)
    everything = inputs[...].reshape(copies * pairs, features)
    products[...] = dot(everything, everything, ((1,), (1,)))
    slices[...] = inputs[:, :, pl.ds(pl.multiple_of(core * half, half), half)]
    own[CHUNKS + 3].wait()
    own[CHUNKS + 4].wait()
    gate_value = gates[0].astype(jnp.float32).reshape(pairs, g_ref.shape[-1])
    up_value = gates[1].astype(jnp.float32).reshape(pairs, u_ref.shape[-1])
    own[CHUNKS + 2].wait()
    swaps[1].wait_recv()
    near = pl.ds(0, spots - 1)
    hidden = None
    for h in range(CHUNKS):
        pltpu.make_async_copy(sent.at[h, core, spot], routed.at[spot, :, columns(h)], piece_sem.at[h]).wait()
        remote(
            sent.at[h, 1 - core, spot], routed.at[spot, :, columns(h)], near_send.at[h], near_recv.at[h], partner
        ).wait_recv()
        both = sent.at[h, :, near]
        remote(both, both, plane_send.at[h], plane_recv.at[h], partner).wait_recv()
        for c in range(2):
            here = routed[:, :, pl.ds(c * half + h * width, width)].reshape(pairs, width)
            term = dot(here, down[c, :, pl.ds(h * width, width)], ((1,), (1,)))
            hidden = term if hidden is None else hidden + term
    hidden = hidden / math.sqrt(hidden.shape[1])
    sigmoid = jax.nn.sigmoid(gate_value)
    gate_rows = hidden * up_value * sigmoid * (1.0 + gate_value * (1.0 - sigmoid))
    up_rows = hidden * gate_value * sigmoid
    first = core == 0
    rows[core] = jnp.where(first, gate_rows, up_rows).astype(jnp.bfloat16)
    other[...] = jnp.where(first, up_rows, gate_rows).astype(jnp.bfloat16)
    swapped = remote(other, rows.at[core], pair_send.at[2], pair_recv.at[2], partner)
    swapped.start()

    swapped.wait_recv()

    n = made0.shape[0]
    outs, made, held, ready = (own_out, other_out), (made0, made1), (held0, held1), (ready0, ready1)
    ny = GRID[0]
    group = n // ny
    piece = weights.shape[1] // n
    block = group * piece
    rest = pl.ds(0, n - 1)

    factors[0] = orthogonal_factor(products[...], rows[...].reshape(2 * pairs, rows.shape[2]))
    trade = pltpu.make_async_remote_copy(
        src_ref=factors.at[0], dst_ref=factors.at[1], send_sem=swap_sem.at[0], recv_sem=swap_sem.at[1],
        device_id=partner, device_id_type=MESH,
    )
    trade.start()
    indices.wait()

    for q in range(2):
        pltpu.make_async_copy(gate_ref, weights.at[q], load.at[q]).wait()
        if q:
            trade.wait_recv()

        def spread(k, carry, q=q):
            to = shifted(me, k)
            pltpu.make_async_remote_copy(
                src_ref=made[q].at[to], dst_ref=held[q].at[me], send_sem=send.at[q], recv_sem=recv.at[q],
                device_id={"ep": to}, device_id_type=MESH,
            ).start()
            return carry

        def produce(dy, carry, q=q):
            y = lax.rem(me // group + dy, ny)
            span = pl.ds(pl.multiple_of(y * block, block), block)
            ortho = dot(slices[:, :, span].reshape(2 * pairs, block), factors[q], ((0,), (0,)))
            fresh = (weights[q, span, :].astype(jnp.float32) - factor * ortho).astype(jnp.bfloat16)
            made[q][pl.ds(y * group, group)] = fresh.reshape(group, piece, fresh.shape[1])
            lax.fori_loop(jnp.where(dy == 0, 1, dy * group), (dy + 1) * group, spread, 0)
            return carry

        lax.fori_loop(0, ny, produce, 0)
        pltpu.make_async_copy(made[q].at[me], held[q].at[me], local.at[q]).start()

    for q in range(2):
        pltpu.make_async_copy(made[q].at[me], held[q].at[me], local.at[q]).wait()
        pltpu.make_async_remote_copy(
            src_ref=made[q].at[rest], dst_ref=held[q].at[rest], send_sem=send.at[q], recv_sem=recv.at[q],
            device_id={"ep": shifted(me, 1)}, device_id_type=MESH,
        ).wait_recv()

        def collect(k, carry, q=q):
            to = shifted(me, k)
            ready[q][k] = held[q][inverse[0, to]]
            pltpu.make_async_remote_copy(
                src_ref=ready[q].at[k], dst_ref=outs[q].at[me], send_sem=send.at[2 + q], recv_sem=recv.at[2 + q],
                device_id={"ep": to}, device_id_type=MESH,
            ).start()
            return carry

        lax.fori_loop(1, n, collect, 0)
        ready[q][0] = held[q][inverse[0, me]]
        pltpu.make_async_copy(ready[q].at[0], outs[q].at[me], local.at[2 + q]).start()

    trade.wait_send()
    for q in range(2):
        pltpu.make_async_copy(ready[q].at[0], outs[q].at[me], local.at[2 + q]).wait()
        pltpu.make_async_remote_copy(
            src_ref=made[q].at[rest], dst_ref=held[q].at[rest], send_sem=send.at[q], recv_sem=recv.at[q],
            device_id={"ep": shifted(me, 1)}, device_id_type=MESH,
        ).wait_send()
        last = pltpu.make_async_remote_copy(
            src_ref=ready[q].at[rest], dst_ref=outs[q].at[rest], send_sem=send.at[2 + q], recv_sem=recv.at[2 + q],
            device_id={"ep": shifted(me, 1)}, device_id_type=MESH,
        )
        last.wait_send()
        last.wait_recv()

    all_keys.wait_send()
    for swap in swaps:
        swap.wait_send()
    for h in range(CHUNKS):
        remote(line.at[h, others], line.at[h, others], line_send.at[h], line_recv.at[h], above(1)).wait_send()
        remote(
            sent.at[h, 1 - core, spot], routed.at[spot, :, columns(h)], near_send.at[h], near_recv.at[h], partner
        ).wait_send()
        both = sent.at[h, :, near]
        remote(both, both, plane_send.at[h], plane_recv.at[h], partner).wait_send()
    swapped.wait_send()


def step(factor, ids, copies, probs, inverse, dy, inputs, gate, up, down, gate_matrix, up_matrix):
    top = ids.shape[0]
    pairs, features = inputs.shape[0] * inputs.shape[1], inputs.shape[2]
    inner, half = down.shape
    tokens = dy.shape[0]
    nz, spots = GRID[2], GRID[0] * GRID[1]
    slots = pairs // spots
    width = half // CHUNKS
    everywhere = pl.BlockSpec(memory_space=pl.ANY)
    bf16 = jnp.bfloat16
    experts = inverse.shape[1]
    shape = jax.ShapeDtypeStruct((experts, half // experts, inner), bf16)
    semaphores = pltpu.SemaphoreType.DMA
    return pl.pallas_call(
        functools.partial(step_kernel, top, factor),
        out_shape=(shape, shape),
        in_specs=[everywhere] * 11,
        out_specs=(everywhere, everywhere),
        scratch_shapes=[
            pltpu.VMEM(ids.shape, jnp.int32),
            pltpu.VMEM(ids.shape, jnp.int32),
            pltpu.VMEM(ids.shape, jnp.float32),
            pltpu.VMEM((2 * pairs, 2 * pairs), jnp.float32),
            pltpu.VMEM((2, pairs, half), bf16),
            pltpu.VMEM((CHUNKS, nz, tokens, width), bf16),
            pltpu.VMEM((2 * top, 128), jnp.float32),
            pltpu.VMEM((2,) + gate.shape, bf16),
            pltpu.VMEM((nz, 2 * top, 128), jnp.float32),
            pltpu.VMEM((CHUNKS, 2, spots, slots, width), bf16),
            pltpu.VMEM((spots, slots, features), bf16),
            pltpu.VMEM((2,) + inputs.shape, bf16),
            pltpu.VMEM((2, pairs, features), bf16),
            pltpu.VMEM((2, inner, half), bf16),
            pltpu.VMEM((2, pairs, inner), bf16),
            pltpu.VMEM((pairs, inner), bf16),
            semaphores((CHUNKS,)),
            semaphores((CHUNKS,)),
            semaphores((2,)),
            semaphores((CHUNKS,)),
            semaphores((CHUNKS,)),
            semaphores((CHUNKS,)),
            semaphores((CHUNKS,)),
            semaphores((3,)),
            semaphores((3,)),
            semaphores((CHUNKS + 5,)),
            semaphores((CHUNKS,)),
            semaphores((3,)),
            pltpu.SMEM(inverse.shape, jnp.int32),
            pltpu.VMEM((2, half, inner), bf16),
            pltpu.VMEM((2, 2 * pairs, inner), bf16),
        ]
        + [pltpu.VMEM(shape.shape, bf16)] * 6
        + [
            semaphores((2,)),
            semaphores((4,)),
            semaphores((4,)),
            semaphores((4,)),
            semaphores((2,)),
            semaphores,
        ],
        compiler_params=pltpu.CompilerParams(
            collective_id=1, has_side_effects=True, vmem_limit_bytes=60 * 2**20
        ),
        name="step",
    )(ids, copies, probs, inverse, dy, inputs, gate, up, down, gate_matrix, up_matrix)


def shards(
    dy,
    probs,
    expert_ids,
    copy_choice,
    saved_inputs,
    saved_gate,
    saved_up,
    down_weight,
    gate_weight,
    up_weight,
    new_owner,
):
    first = lax.axis_index("rep") == 0
    experts = lax.axis_size("ep")
    width = dy.shape[1]
    inner = saved_gate.shape[4]
    half = width // 2
    expert = jnp.arange(experts, dtype=jnp.int32)
    inverse = jnp.sum(
        jnp.where(new_owner[:, None] == expert[None, :], expert[:, None], 0), axis=0, dtype=jnp.int32
    ).reshape(1, experts)
    own, other = step(
        step_scale * math.sqrt(width), expert_ids.T, copy_choice.T, probs.T, inverse, dy,
        saved_inputs[0, 0], saved_gate[0, 0], saved_up[0, 0], down_weight[0], gate_weight[0], up_weight[0],
    )
    new_gate, new_up = jnp.where(first, own, other), jnp.where(first, other, own)
    return new_gate.reshape(1, half, inner), new_up.reshape(1, half, inner)


def solution(mesh):
    in_specs = (
        P("ep", None),
        P("ep", None),
        P("ep", None),
        P("ep", None),
        P("ep", "rep", None, None, None),
        P("ep", "rep", None, None, None),
        P("ep", "rep", None, None, None),
        P("ep", None, "rep"),
        P("ep", "rep", None),
        P("ep", "rep", None),
        P(),
    )
    out_specs = (P("ep", "rep", None), P("ep", "rep", None))
    return jax.shard_map(shards, mesh=mesh, in_specs=in_specs, out_specs=out_specs, check_vma=False)
```
